32 devices in a mesh: head: 2 (over y), seq: 16 (over z, x, core).
Axes of the slice: x: 2, y: 2, z: 4, core: 2. Of those that a mesh axis runs over, the one named last changes fastest.
Arguments:
- tokens: bfloat16 [4096, 3072], P(('seq', 'head')), may hold values from -48 to 48
- segment_ids: int32 [4096], replicated, may hold values from 0 to 15, as said below
- lengths: int32 [16], replicated, may hold values from 1 to 1024, as said below
- deal: int32 [16], replicated, may hold values from 0 to 15, each once
- attn_gain: float32 [3072], replicated, may hold values from 0.25 to 1.75
- query_key_value_weight: bfloat16 [3072, 5120], P(None, 'head'), may hold values from -4 to 4
- out_weight: bfloat16 [3072, 3072], P('head'), may hold values from -0.109375 to 0.109375
- mlp_gain: float32 [3072], replicated, may hold values from 0.25 to 1.75
- gate_up_weight: bfloat16 [3072, 2, 4096], P('seq', None, 'head'), may hold values from -0.109375 to 0.109375
- down_weight: bfloat16 [3072, 4096], P('seq', 'head'), may hold values from -0.09375 to 0.09375
Outputs:
- out: bfloat16 [4096, 3072], P(('seq', 'head'))
- key_cache: bfloat16 [8, 4096, 128], P('head', 'seq')
- value_cache: bfloat16 [8, 4096, 128], P('head', 'seq')
The draws below stay inside these ranges and needn't reach their ends.
Inputs may be any that keep to these rules, and one draw needn't show every extreme that they name: lengths[s] is the number of stream tokens of prompt s; they sum to 4096 and the longest is exactly 1024. segment_ids[p] is the prompt holding stream position p; prompts 0 to 15 lie end to end in order with the lengths given by lengths. `deal`: each block number appears once.
All inputs are finite; a program needn't handle non-finite values.
Results may differ from the reference program's by a relative error of at most 0.011.
Values may be sent and summed in bfloat16 or wider, within the bound.
A program may use at most 192 MiB of HBM per device.

```python
import math
import jax
import jax.numpy as jnp
from jax import lax

MODEL_WIDTH = 3072
QUERY_HEAD_COUNT = 24
KEY_VALUE_HEADS = 8
HEAD_WIDTH = 128
FFW = 4096
BLK = 256
PROMPTS = 16
BLOCKS = 16
STREAM_LENGTH = 4096
MOSTLEN = 1024


def prompt_table(key):
    base_rows = (STREAM_LENGTH - MOSTLEN) // (PROMPTS - 1)
    remainder = STREAM_LENGTH - MOSTLEN - base_rows * (PROMPTS - 1)
    spread = base_rows * 3 // 8
    jitter = jax.random.randint(jax.random.fold_in(key, 11), (PROMPTS - 1,), -spread, spread + 1)
    others = base_rows + jitter - jnp.roll(jitter, 1)
    others = others + jnp.where(jnp.arange(PROMPTS - 1) == 0, remainder, 0)
    longest = jax.random.randint(jax.random.fold_in(key, 12), (), 0, PROMPTS)
    prompt_index = jnp.arange(PROMPTS)
    shifted = jnp.clip(prompt_index - (prompt_index > longest).astype(jnp.int32), 0, PROMPTS - 2)
    picked = jnp.take(others, shifted)
    return jnp.where(prompt_index == longest, MOSTLEN, picked).astype(jnp.int32)


def draw_lengths(key, part):
    return prompt_table(key)


def draw_segment_ids(key, part):
    prompt_ends = jnp.cumsum(prompt_table(key)).astype(jnp.int32)
    stream_index = jnp.arange(STREAM_LENGTH, dtype=jnp.int32)
    return jnp.sum((stream_index[None, :] >= prompt_ends[:, None]).astype(jnp.int32), axis=0).astype(jnp.int32)


def draw_tokens(key, part):
    base_rows = jnp.clip(jax.random.normal(jax.random.fold_in(key, 1), (STREAM_LENGTH, MODEL_WIDTH), jnp.float32), -5.0, 5.0)
    row_scale = jnp.exp(jax.random.uniform(jax.random.fold_in(key, 2), (STREAM_LENGTH, 1), jnp.float32, math.log(0.4), math.log(4.0)))
    column_scale = jnp.exp(jax.random.uniform(jax.random.fold_in(key, 3), (1, MODEL_WIDTH), jnp.float32, math.log(0.5), math.log(2.0)))
    return (base_rows * row_scale * column_scale).astype(jnp.bfloat16)


def draw_query_key_value_weight(key, part):
    heads_per_group = QUERY_HEAD_COUNT // KEY_VALUE_HEADS
    scale_of_weight = 1.2 / math.sqrt(MODEL_WIDTH)
    unrotated_part = jnp.clip(jax.random.normal(jax.random.fold_in(key, 20), (MODEL_WIDTH, KEY_VALUE_HEADS, heads_per_group + 2, HEAD_WIDTH), jnp.float32), -6.0, 6.0) * scale_of_weight
    unrotated_part = jnp.clip(unrotated_part, -4.0, 4.0)
    return unrotated_part.reshape(MODEL_WIDTH, KEY_VALUE_HEADS * (heads_per_group + 2) * HEAD_WIDTH).astype(jnp.bfloat16)


def levels(key, shape, pieces, least, high):
    def one(dim, shards_of):
        heights = jax.random.uniform(jax.random.fold_in(jax.random.fold_in(key, 6), dim), (shards_of,), jnp.float32, least / len(pieces), high / len(pieces))
        return jnp.repeat(jnp.exp(heights), shape[dim] // shards_of).reshape((-1,) + (1,) * (len(shape) - dim - 1))

    level = one(*pieces[0])
    for cut in pieces[1:]:
        level = level * one(*cut)
    return level


def gaussian(key, extent, scale, bound, shards=(), kind=jnp.bfloat16):
    array = scale * jax.random.normal(key, extent, jnp.float32)
    if shards:
        array = array * levels(key, extent, shards, -0.22, 0.18)
    return jnp.clip(array, -bound, bound).astype(kind)


def setup_inputs(seed: int = 0) -> dict:
    keys = jax.random.split(jax.random.key(seed), 11)
    tokens = draw_tokens(jax.random.fold_in(keys[10], 71), 0)
    segment_ids = draw_segment_ids(jax.random.fold_in(keys[10], 71), 0)
    lengths = draw_lengths(jax.random.fold_in(keys[10], 71), 0)
    deal = jax.random.permutation(keys[3], BLOCKS).astype(jnp.int32)
    attn_gain = jnp.clip(1.0 + 0.15 * jax.random.normal(keys[4], (MODEL_WIDTH,), jnp.float32), 0.25, 1.75)
    query_key_value_weight = draw_query_key_value_weight(jax.random.fold_in(keys[10], 71), 0)
    out_weight = gaussian(keys[6], (QUERY_HEAD_COUNT * HEAD_WIDTH, MODEL_WIDTH), (QUERY_HEAD_COUNT * HEAD_WIDTH) ** -0.5, 0.109375, ((0, 2),))
    mlp_gain = jnp.clip(1.0 + 0.15 * jax.random.normal(keys[7], (MODEL_WIDTH,), jnp.float32), 0.25, 1.75)
    gate_up_weight = gaussian(keys[8], (MODEL_WIDTH, 2, FFW), MODEL_WIDTH ** -0.5, 0.109375, ((0, 16), (2, 2)))
    down_weight = gaussian(keys[9], (MODEL_WIDTH, FFW), FFW ** -0.5, 0.09375, ((0, 16), (1, 2)))
    return {"tokens": tokens, "segment_ids": segment_ids, "lengths": lengths, "deal": deal, "attn_gain": attn_gain, "query_key_value_weight": query_key_value_weight, "out_weight": out_weight, "mlp_gain": mlp_gain, "gate_up_weight": gate_up_weight, "down_weight": down_weight}


EPSILON = 1e-05
ROPE_BASE = 500000.0

def frequencies(head_size):
    exponent = jnp.arange(0, head_size, 2, dtype=jnp.float32) / head_size
    inverse = 1.0 / ROPE_BASE ** exponent
    wavelength = 2.0 * math.pi / inverse
    smooth = (8192.0 / wavelength - 1.0) / 3.0
    blended = (1.0 - smooth) * inverse / 32.0 + smooth * inverse
    return jnp.where(wavelength > 8192.0, inverse / 32.0, jnp.where(wavelength < 2048.0, inverse, blended))

def rotate(row_values, position, inverse):
    angles = position.astype(jnp.float32)[:, None] * inverse[None, :]
    cosine = jnp.cos(angles)[:, None, None, :]
    sine_term = jnp.sin(angles)[:, None, None, :]
    half_size = row_values.shape[-1] // 2
    first_half = row_values[..., :half_size]
    second_half = row_values[..., half_size:]
    return jnp.concatenate([first_half * cosine - second_half * sine_term, second_half * cosine + first_half * sine_term], axis=-1)

def normalize(row_values, gain_vector):
    values_wide = row_values.astype(jnp.float32)
    factor = lax.rsqrt(lax.optimization_barrier(jnp.mean(values_wide * values_wide, axis=-1, keepdims=True)) + EPSILON)
    return (values_wide * factor * gain_vector.astype(jnp.float32)).astype(jnp.bfloat16)

def reference(tokens, segment_ids, lengths, deal, attn_gain, query_key_value_weight, out_weight, mlp_gain, gate_up_weight, down_weight):
    heads_per_group = QUERY_HEAD_COUNT // KEY_VALUE_HEADS
    row_index = jnp.arange(STREAM_LENGTH, dtype=jnp.int32)
    stream_of_row = (jnp.take(deal, row_index // BLK) * BLK + row_index % BLK).astype(jnp.int32)
    stream_tokens = jnp.zeros_like(tokens).at[stream_of_row].set(tokens)
    starts = (jnp.cumsum(lengths) - lengths).astype(jnp.int32)
    rope_pos = (row_index - jnp.take(starts, segment_ids)).astype(jnp.int32)
    normalized_rows = normalize(stream_tokens, attn_gain)
    projected_rows = jnp.dot(normalized_rows, query_key_value_weight, preferred_element_type=jnp.float32).reshape(STREAM_LENGTH, KEY_VALUE_HEADS, heads_per_group + 2, HEAD_WIDTH)
    inverse = frequencies(HEAD_WIDTH)
    queries = rotate(projected_rows[:, :, :heads_per_group], rope_pos, inverse).astype(jnp.bfloat16)
    key_matrix = rotate(projected_rows[:, :, heads_per_group:heads_per_group + 1], rope_pos, inverse)[:, :, 0].astype(jnp.bfloat16)
    value_matrix = projected_rows[:, :, heads_per_group + 1].astype(jnp.bfloat16)
    qblock = math.gcd(STREAM_LENGTH, 512)
    backward_reach = MOSTLEN
    padded_keys = jnp.concatenate([jnp.zeros((backward_reach, KEY_VALUE_HEADS, HEAD_WIDTH), jnp.bfloat16), key_matrix], axis=0)
    padded_values = jnp.concatenate([jnp.zeros((backward_reach, KEY_VALUE_HEADS, HEAD_WIDTH), jnp.bfloat16), value_matrix], axis=0)
    pad_segments = jnp.concatenate([jnp.full((backward_reach,), -1, jnp.int32), segment_ids.astype(jnp.int32)], axis=0)
    pad_positions = jnp.arange(STREAM_LENGTH + backward_reach, dtype=jnp.int32) - backward_reach
    score_scale = 1.0 / math.sqrt(HEAD_WIDTH)

    def one_block(block_number):
        first_row = (block_number * qblock).astype(jnp.int32)
        window = qblock + backward_reach
        query_block = lax.dynamic_slice_in_dim(queries, first_row, qblock, 0).astype(jnp.float32)
        key_block = lax.dynamic_slice_in_dim(padded_keys, first_row, window, 0).astype(jnp.float32)
        value_block = lax.dynamic_slice_in_dim(padded_values, first_row, window, 0).astype(jnp.float32)
        key_segments = lax.dynamic_slice_in_dim(pad_segments, first_row, window, 0)
        key_positions = lax.dynamic_slice_in_dim(pad_positions, first_row, window, 0)
        query_segments = lax.dynamic_slice_in_dim(segment_ids.astype(jnp.int32), first_row, qblock, 0)
        query_positions = first_row + jnp.arange(qblock, dtype=jnp.int32)
        visible = (query_segments[:, None] == key_segments[None, :]) & (key_positions[None, :] <= query_positions[:, None])
        scores = jnp.einsum('qgjd,kgd->gjqk', query_block, key_block) * score_scale
        masked = jnp.where(visible, scores, -1e+30)
        row_max = lax.optimization_barrier(jnp.max(masked, axis=-1))
        weights = jnp.where(visible, jnp.exp(masked - row_max[..., None]), 0.0)
        row_total = lax.optimization_barrier(jnp.sum(weights, axis=-1))
        rounded = lax.optimization_barrier(weights.astype(jnp.bfloat16)).astype(jnp.float32)
        attention_block = jnp.einsum('gjqk,kgd->qgjd', rounded, value_block)
        attention_block = attention_block / jnp.transpose(row_total, (2, 0, 1))[..., None]
        return attention_block.astype(jnp.bfloat16).reshape(qblock, QUERY_HEAD_COUNT * HEAD_WIDTH)
    attended = lax.map(one_block, jnp.arange(STREAM_LENGTH // qblock, dtype=jnp.int32)).reshape(STREAM_LENGTH, QUERY_HEAD_COUNT * HEAD_WIDTH)
    residual = (stream_tokens.astype(jnp.float32) + jnp.dot(attended, out_weight, preferred_element_type=jnp.float32)).astype(jnp.bfloat16)
    mlp_in = normalize(residual, mlp_gain)
    gate_value = jnp.dot(mlp_in, gate_up_weight[:, 0, :], preferred_element_type=jnp.float32)
    up_value = jnp.dot(mlp_in, gate_up_weight[:, 1, :], preferred_element_type=jnp.float32)
    hidden = (jax.nn.silu(gate_value) * up_value).astype(jnp.bfloat16)
    down_value = jnp.dot(hidden, down_weight.T, preferred_element_type=jnp.float32)
    stream_out = (residual.astype(jnp.float32) + down_value).astype(jnp.bfloat16)
    out = jnp.take(stream_out, stream_of_row, axis=0)
    key_cache = jnp.transpose(jnp.take(key_matrix, stream_of_row, axis=0), (1, 0, 2))
    value_cache = jnp.transpose(jnp.take(value_matrix, stream_of_row, axis=0), (1, 0, 2))
    return (out, key_cache, value_cache)
```

```python
import functools
import math

import jax
import jax.numpy as jnp
from jax import lax
from jax.experimental import pallas as pl
from jax.experimental.pallas import tpu as pltpu
from jax.sharding import PartitionSpec as P

QUERY_HEAD_COUNT = 24
KEY_VALUE_HEADS = 8
HEAD_WIDTH = 128


EPSILON = 1e-05
ROPE_BASE = 500000.0


def frequencies(head_size):
    exponent = jnp.arange(0, head_size, 2, dtype=jnp.float32) / head_size
    inverse = 1.0 / ROPE_BASE**exponent
    wavelength = 2.0 * math.pi / inverse
    smooth = (8192.0 / wavelength - 1.0) / 3.0
    blended = (1.0 - smooth) * inverse / 32.0 + smooth * inverse
    return jnp.where(
        wavelength > 8192.0, inverse / 32.0, jnp.where(wavelength < 2048.0, inverse, blended)
    )


def rotate(row_values, position, inverse):
    angles = position.astype(jnp.float32)[:, None] * inverse[None, :]
    cosine = jnp.cos(angles)[:, None, None, :]
    sine_term = jnp.sin(angles)[:, None, None, :]
    half_size = row_values.shape[-1] // 2
    first_half = row_values[..., :half_size]
    second_half = row_values[..., half_size:]
    return jnp.concatenate(
        [
            first_half * cosine - second_half * sine_term,
            second_half * cosine + first_half * sine_term,
        ],
        axis=-1,
    )


def normalize(row_values, gain_vector):
    values_wide = row_values.astype(jnp.float32)
    factor = lax.rsqrt(jnp.mean(values_wide * values_wide, axis=-1, keepdims=True) + EPSILON)
    return (values_wide * factor * gain_vector).astype(jnp.bfloat16)


def down_product(hidden, down_rows):
    return lax.dot_general(
        hidden, down_rows, (((1,), (1,)), ((), ())), preferred_element_type=jnp.float32
    )


def shift(values, step, count):
    return lax.ppermute(values, "head", [(i, (i + step) % count) for i in range(count)])


def gather_kernel(levels, own_ref, out_ref, copy_sem, up_sem, down_sem, side_sem, core_sem, recv_sem):
    me = lax.axis_index("seq")
    core = me % 2
    side = (me // 2) % 2
    level = me // 4
    has_above = level < levels - 1
    has_below = level > 0

    def slot(at_level, at_side, at_core):
        return at_level * 4 + at_side * 2 + at_core

    up = me + 4
    down = me - 4
    across = me + 2 - 4 * side
    partner = me + 1 - 2 * core

    def copy(source, index, send_sem, target):
        return pltpu.make_async_remote_copy(
            src_ref=source,
            dst_ref=out_ref.at[index],
            send_sem=send_sem,
            recv_sem=recv_sem.at[index],
            device_id={"seq": target},
            device_id_type=pl.DeviceIdType.MESH,
        )

    def arrived(index):
        copy(out_ref.at[index], index, copy_sem, partner).wait_recv()

    def greet(target):
        pl.semaphore_signal(
            barrier, inc=1, device_id={"seq": target}, device_id_type=pl.DeviceIdType.MESH
        )

    barrier = pltpu.get_barrier_semaphore()
    greet(partner)
    greet(across)
    pl.when(has_above)(lambda: greet(up))
    pl.when(has_below)(lambda: greet(down))
    peers = 2 + jnp.where(has_above, 1, 0) + jnp.where(has_below, 1, 0)
    pl.semaphore_wait(barrier, peers)

    pl.when(has_above)(lambda: copy(own_ref, me, up_sem.at[0], up).start())
    pl.when(has_below)(lambda: copy(own_ref, me, down_sem.at[0], down).start())
    copy(own_ref, me, side_sem.at[0], across).start()
    copy(own_ref, me, core_sem.at[0], partner).start()
    keep = pltpu.make_async_copy(own_ref, out_ref.at[me], copy_sem)
    keep.start()

    for far in range(1, levels):

        @pl.when(level - far >= 0)
        def _():
            index = slot(level - far, side, core)
            arrived(index)
            block = out_ref.at[index]
            pl.when(has_above)(lambda: copy(block, index, up_sem.at[far], up).start())
            copy(block, index, side_sem.at[2 * far - 1], across).start()
            copy(block, index, core_sem.at[2 * far - 1], partner).start()

        @pl.when(level + far < levels)
        def _():
            index = slot(level + far, side, core)
            arrived(index)
            block = out_ref.at[index]
            pl.when(has_below)(lambda: copy(block, index, down_sem.at[far], down).start())
            copy(block, index, side_sem.at[2 * far], across).start()
            copy(block, index, core_sem.at[2 * far], partner).start()

    offset = 2 * levels - 1

    def pass_on(at_level, number):
        index = slot(at_level, 1 - side, core)
        arrived(index)
        copy(out_ref.at[index], index, core_sem.at[offset + number], partner).start()

    pass_on(level, 0)
    for far in range(1, levels):
        pl.when(level - far >= 0)(lambda: pass_on(level - far, 2 * far - 1))
        pl.when(level + far < levels)(lambda: pass_on(level + far, 2 * far))

    for at_level in range(levels):
        for at_side in range(2):
            arrived(slot(at_level, at_side, 1 - core))

    keep.wait()

    def sent(sem, target):
        copy(own_ref, me, sem, target).wait_send()

    pl.when(has_above)(lambda: sent(up_sem.at[0], up))
    pl.when(has_below)(lambda: sent(down_sem.at[0], down))
    sent(side_sem.at[0], across)
    sent(core_sem.at[0], partner)
    sent(core_sem.at[offset], partner)
    for far in range(1, levels):

        @pl.when(level - far >= 0)
        def _():
            pl.when(has_above)(lambda: sent(up_sem.at[far], up))
            sent(side_sem.at[2 * far - 1], across)
            sent(core_sem.at[2 * far - 1], partner)
            sent(core_sem.at[offset + 2 * far - 1], partner)

        @pl.when(level + far < levels)
        def _():
            pl.when(has_below)(lambda: sent(down_sem.at[far], down))
            sent(side_sem.at[2 * far], across)
            sent(core_sem.at[2 * far], partner)
            sent(core_sem.at[offset + 2 * far], partner)


def gather_blocks(own, count):
    levels = count // 4
    dma = pltpu.SemaphoreType.DMA
    return pl.pallas_call(
        functools.partial(gather_kernel, levels),
        out_shape=jax.ShapeDtypeStruct((count,) + own.shape, own.dtype),
        in_specs=[pl.BlockSpec(memory_space=pl.ANY)],
        out_specs=pl.BlockSpec(memory_space=pl.ANY),
        scratch_shapes=[
            dma,
            dma((levels,)),
            dma((levels,)),
            dma((2 * levels - 1,)),
            dma((2 * (2 * levels - 1),)),
            dma((count,)),
        ],
        compiler_params=pltpu.CompilerParams(collective_id=0, has_side_effects=True),
        cost_estimate=pl.CostEstimate(flops=0, bytes_accessed=count * own.size * 2, transcendentals=0),
    )(own)


def attention_kernel(window, table_ref, start_ref, query_ref, *refs):
    keys = refs[:window]
    values = refs[window : 2 * window]
    out_ref = refs[2 * window]
    block = keys[0].shape[-2]
    query = query_ref[0]
    heads = query.shape[0] // block
    local = jnp.concatenate([start_ref[...]] * heads, axis=0)
    row = lax.broadcasted_iota(jnp.int32, (block, 1), 0)
    row = jnp.concatenate([row] * heads, axis=0)
    key_all = jnp.concatenate([ref[0, 0, 0] for ref in keys], axis=0)
    value_all = jnp.concatenate([ref[0, 0, 0] for ref in values], axis=0)
    scores = lax.dot_general(
        query, key_all, (((1,), (1,)), ((), ())), preferred_element_type=jnp.float32
    ) * (1.0 / math.sqrt(HEAD_WIDTH))
    column = lax.broadcasted_iota(jnp.int32, scores.shape, 1)
    visible = (column >= local) & (column <= row + (window - 1) * block)
    masked = jnp.where(visible, scores, -1e30)
    top = jnp.max(masked, axis=1, keepdims=True)
    weights = jnp.exp(masked - top)
    total = jnp.sum(weights, axis=1, keepdims=True)
    mixed = jnp.dot(weights.astype(jnp.bfloat16), value_all, preferred_element_type=jnp.float32)
    out_ref[0] = (mixed / total).astype(jnp.bfloat16)


def attend(query_heads, pieces, table, local_starts, window):
    groups, rows, width = query_heads.shape
    block = local_starts.shape[0]

    def spec(kind, back):
        return pl.BlockSpec(
            (1, 1, 1, block, width),
            lambda g, table_ref: (table_ref[back], kind, g, 0, 0),
        )

    flops = 4 * groups * rows * window * block * width
    return pl.pallas_call(
        functools.partial(attention_kernel, window),
        grid_spec=pltpu.PrefetchScalarGridSpec(
            num_scalar_prefetch=1,
            grid=(groups,),
            in_specs=[
                pl.BlockSpec((block, 1), lambda g, *_: (0, 0)),
                pl.BlockSpec((1, rows, width), lambda g, *_: (g, 0, 0)),
            ]
            + [spec(0, back) for back in range(window)]
            + [spec(1, back) for back in range(window)],
            out_specs=pl.BlockSpec((1, rows, width), lambda g, *_: (g, 0, 0)),
        ),
        out_shape=jax.ShapeDtypeStruct(query_heads.shape, jnp.bfloat16),
        compiler_params=pltpu.CompilerParams(vmem_limit_bytes=48 * 1024 * 1024),
        cost_estimate=pl.CostEstimate(
            flops=flops,
            bytes_accessed=groups * (rows * 2 + window * block * 2) * width * 2,
            transcendentals=groups * rows * window * block,
        ),
    )(table, local_starts, query_heads, *([pieces] * (2 * window)))


def shards(
    tokens,
    segment_ids,
    lengths,
    deal,
    attn_gain,
    query_key_value_weight,
    out_weight,
    mlp_gain,
    gate_up_weight,
    down_weight,
):
    head_count = lax.axis_size("head")
    head_index = lax.axis_index("head")
    seq_index = lax.axis_index("seq")
    rows_here = tokens.shape[0]
    block_rows = rows_here * head_count
    heads_per_group = QUERY_HEAD_COUNT // KEY_VALUE_HEADS
    groups = query_key_value_weight.shape[1] // ((heads_per_group + 2) * HEAD_WIDTH)
    blocks = deal.shape[0]
    longest = segment_ids.shape[0] // 4
    window = min(blocks, -(-(longest - 1) // block_rows) + 1)
    hidden_here = gate_up_weight.shape[2]
    weight_rows = jnp.concatenate(
        [gate_up_weight.reshape(gate_up_weight.shape[0], 2 * hidden_here), down_weight], axis=1
    )
    weights_all = lax.all_gather(weight_rows, "seq", axis=0, tiled=True)
    block_ids = jnp.arange(blocks, dtype=jnp.int32)
    my_block = jnp.sum(jnp.where(block_ids == seq_index, deal, 0))
    stream_pos = my_block * block_rows + jnp.arange(block_rows, dtype=jnp.int32)
    query_segments = lax.dynamic_slice_in_dim(segment_ids, my_block * block_rows, block_rows, 0)
    prompts = jnp.arange(lengths.shape[0], dtype=jnp.int32)
    starts = jnp.sum(jnp.where(prompts[None, :] < prompts[:, None], lengths[None, :], 0), axis=1)
    prompt_hits = query_segments[:, None] == jnp.arange(lengths.shape[0], dtype=jnp.int32)[None, :]
    query_starts = jnp.sum(jnp.where(prompt_hits, starts[None, :], 0), axis=1)
    rope_pos = stream_pos - query_starts
    wanted = jnp.maximum(my_block - (window - 1) + jnp.arange(window, dtype=jnp.int32), 0)
    table = jnp.sum(
        jnp.where(wanted[:, None] == deal[None, :], block_ids[None, :], 0), axis=1
    ).astype(jnp.int32)
    local_starts = (query_starts - (my_block - (window - 1)) * block_rows)[:, None]
    inverse = frequencies(HEAD_WIDTH)
    full_rows = jnp.zeros((block_rows, tokens.shape[1]), tokens.dtype)
    full_rows = lax.dynamic_update_slice_in_dim(full_rows, tokens, head_index * rows_here, 0)
    for step in range(1, head_count):
        source = (head_index - step) % head_count
        full_rows = lax.dynamic_update_slice_in_dim(
            full_rows, shift(tokens, step, head_count), source * rows_here, 0
        )
    projected_rows = jnp.dot(
        normalize(full_rows, attn_gain), query_key_value_weight, preferred_element_type=jnp.float32
    )
    projected_rows = projected_rows.reshape(block_rows, groups, heads_per_group + 2, HEAD_WIDTH)
    queries = rotate(projected_rows[:, :, :heads_per_group], rope_pos, inverse).astype(jnp.bfloat16)
    key_matrix = rotate(
        projected_rows[:, :, heads_per_group : heads_per_group + 1], rope_pos, inverse
    )[:, :, 0].astype(jnp.bfloat16)
    value_matrix = projected_rows[:, :, heads_per_group + 1].astype(jnp.bfloat16)
    key_cache = jnp.transpose(key_matrix, (1, 0, 2))
    value_cache = jnp.transpose(value_matrix, (1, 0, 2))
    query_heads = jnp.transpose(queries, (1, 2, 0, 3)).reshape(
        groups, heads_per_group * block_rows, HEAD_WIDTH
    )
    key_value = jnp.stack([key_cache, value_cache])
    pieces = gather_blocks(key_value, blocks)
    attended = attend(query_heads, pieces, table, local_starts, window)
    attended = jnp.transpose(
        attended.reshape(groups, heads_per_group, block_rows, HEAD_WIDTH), (2, 0, 1, 3)
    ).reshape(block_rows, groups * heads_per_group * HEAD_WIDTH)
    part = jnp.dot(attended, out_weight, preferred_element_type=jnp.float32).astype(jnp.bfloat16)
    total_proj = part.astype(jnp.float32)
    for step in range(1, head_count):
        total_proj = total_proj + shift(part, step, head_count).astype(jnp.float32)
    full_residual = (full_rows.astype(jnp.float32) + total_proj).astype(jnp.bfloat16)
    mlp_in = lax.optimization_barrier(normalize(full_residual, mlp_gain))
    residual = lax.dynamic_slice_in_dim(full_residual, head_index * rows_here, rows_here, 0)
    gate = jnp.dot(mlp_in, weights_all[:, :hidden_here], preferred_element_type=jnp.float32)
    up = jnp.dot(
        mlp_in, weights_all[:, hidden_here : 2 * hidden_here], preferred_element_type=jnp.float32
    )
    hidden = (jax.nn.silu(gate) * up).astype(jnp.bfloat16)
    chunks = []
    pieces_down = 3
    width = weights_all.shape[0] // pieces_down
    for number in range(pieces_down):
        columns = slice(number * width, (number + 1) * width)
        terms = down_product(hidden, weights_all[columns, 2 * hidden_here :]).astype(jnp.bfloat16)
        total = residual[:, columns].astype(jnp.float32) + lax.dynamic_slice_in_dim(
            terms, head_index * rows_here, rows_here, 0
        ).astype(jnp.float32)
        for step in range(1, head_count):
            target = (head_index + step) % head_count
            piece = lax.dynamic_slice_in_dim(terms, target * rows_here, rows_here, 0)
            total = total + shift(piece, step, head_count).astype(jnp.float32)
        chunks.append(total.astype(jnp.bfloat16))
    output = jnp.concatenate(chunks, axis=1)
    return (output, key_cache, value_cache)


def solution(mesh):
    placed = (
        P(("seq", "head"), None),
        P(),
        P(),
        P(),
        P(),
        P(None, "head"),
        P("head", None),
        P(),
        P("seq", None, "head"),
        P("seq", "head"),
    )
    return jax.shard_map(
        shards,
        mesh=mesh,
        in_specs=placed,
        out_specs=(P(("seq", "head"), None), P("head", "seq", None), P("head", "seq", None)),
        check_vma=False,
    )
```

```python
import functools
import math

import jax
import jax.numpy as jnp
from jax import lax
from jax.experimental import pallas as pl
from jax.experimental.pallas import tpu as pltpu
from jax.sharding import PartitionSpec as P

QUERY_HEAD_COUNT = 24
KEY_VALUE_HEADS = 8
HEAD_WIDTH = 128


EPSILON = 1e-05
CORE = 1
SIDE = 2
LEVEL = 4
GROUP = 8
ROPE_BASE = 500000.0


def frequencies(head_size):
    exponent = jnp.arange(0, head_size, 2, dtype=jnp.float32) / head_size
    inverse = 1.0 / ROPE_BASE**exponent
    wavelength = 2.0 * math.pi / inverse
    smooth = (8192.0 / wavelength - 1.0) / 3.0
    blended = (1.0 - smooth) * inverse / 32.0 + smooth * inverse
    return jnp.where(
        wavelength > 8192.0, inverse / 32.0, jnp.where(wavelength < 2048.0, inverse, blended)
    )


def rotate(row_values, position, inverse):
    angles = position.astype(jnp.float32)[:, None] * inverse[None, :]
    cosine = jnp.cos(angles)[:, None, None, :]
    sine_term = jnp.sin(angles)[:, None, None, :]
    half_size = row_values.shape[-1] // 2
    first_half = row_values[..., :half_size]
    second_half = row_values[..., half_size:]
    return jnp.concatenate(
        [
            first_half * cosine - second_half * sine_term,
            second_half * cosine + first_half * sine_term,
        ],
        axis=-1,
    )


def normalize(row_values, gain_vector):
    values_wide = row_values.astype(jnp.float32)
    factor = lax.rsqrt(jnp.mean(values_wide * values_wide, axis=-1, keepdims=True) + EPSILON)
    return (values_wide * factor * gain_vector).astype(jnp.bfloat16)


def down_product(hidden, down_rows):
    return lax.dot_general(
        hidden, down_rows, (((1,), (1,)), ((), ())), preferred_element_type=jnp.float32
    )


def shift(values, step, count):
    return lax.ppermute(values, "head", [(i, (i + step) % count) for i in range(count)])


def gather_kernel(levels, own_ref, out_ref, copy_sem, up_sem, down_sem, side_sem, core_sem, recv_sem):
    me = lax.axis_index("seq")
    core = me % 2
    side = (me // 2) % 2
    level = me // 4
    has_above = level < levels - 1
    has_below = level > 0

    def slot(at_level, at_side, at_core):
        return at_level * 4 + at_side * 2 + at_core

    up = me + 4
    down = me - 4
    across = me + 2 - 4 * side
    partner = me + 1 - 2 * core

    def copy(source, index, send_sem, target):
        return pltpu.make_async_remote_copy(
            src_ref=source,
            dst_ref=out_ref.at[index],
            send_sem=send_sem,
            recv_sem=recv_sem.at[index],
            device_id={"seq": target},
            device_id_type=pl.DeviceIdType.MESH,
        )

    def arrived(index):
        copy(out_ref.at[index], index, copy_sem, partner).wait_recv()

    def greet(target):
        pl.semaphore_signal(
            barrier, inc=1, device_id={"seq": target}, device_id_type=pl.DeviceIdType.MESH
        )

    barrier = pltpu.get_barrier_semaphore()
    greet(partner)
    greet(across)
    pl.when(has_above)(lambda: greet(up))
    pl.when(has_below)(lambda: greet(down))
    peers = 2 + jnp.where(has_above, 1, 0) + jnp.where(has_below, 1, 0)
    pl.semaphore_wait(barrier, peers)

    pl.when(has_above)(lambda: copy(own_ref, me, up_sem.at[0], up).start())
    pl.when(has_below)(lambda: copy(own_ref, me, down_sem.at[0], down).start())
    copy(own_ref, me, side_sem.at[0], across).start()
    copy(own_ref, me, core_sem.at[0], partner).start()
    keep = pltpu.make_async_copy(own_ref, out_ref.at[me], copy_sem)
    keep.start()

    for far in range(1, levels):

        @pl.when(level - far >= 0)
        def _():
            index = slot(level - far, side, core)
            arrived(index)
            block = out_ref.at[index]
            pl.when(has_above)(lambda: copy(block, index, up_sem.at[far], up).start())
            copy(block, index, side_sem.at[2 * far - 1], across).start()
            copy(block, index, core_sem.at[2 * far - 1], partner).start()

        @pl.when(level + far < levels)
        def _():
            index = slot(level + far, side, core)
            arrived(index)
            block = out_ref.at[index]
            pl.when(has_below)(lambda: copy(block, index, down_sem.at[far], down).start())
            copy(block, index, side_sem.at[2 * far], across).start()
            copy(block, index, core_sem.at[2 * far], partner).start()

    offset = 2 * levels - 1

    def pass_on(at_level, number):
        index = slot(at_level, 1 - side, core)
        arrived(index)
        copy(out_ref.at[index], index, core_sem.at[offset + number], partner).start()

    pass_on(level, 0)
    for far in range(1, levels):
        pl.when(level - far >= 0)(lambda: pass_on(level - far, 2 * far - 1))
        pl.when(level + far < levels)(lambda: pass_on(level + far, 2 * far))

    for at_level in range(levels):
        for at_side in range(2):
            arrived(slot(at_level, at_side, 1 - core))

    keep.wait()

    def sent(sem, target):
        copy(own_ref, me, sem, target).wait_send()

    pl.when(has_above)(lambda: sent(up_sem.at[0], up))
    pl.when(has_below)(lambda: sent(down_sem.at[0], down))
    sent(side_sem.at[0], across)
    sent(core_sem.at[0], partner)
    sent(core_sem.at[offset], partner)
    for far in range(1, levels):

        @pl.when(level - far >= 0)
        def _():
            pl.when(has_above)(lambda: sent(up_sem.at[far], up))
            sent(side_sem.at[2 * far - 1], across)
            sent(core_sem.at[2 * far - 1], partner)
            sent(core_sem.at[offset + 2 * far - 1], partner)

        @pl.when(level + far < levels)
        def _():
            pl.when(has_below)(lambda: sent(down_sem.at[far], down))
            sent(side_sem.at[2 * far], across)
            sent(core_sem.at[2 * far], partner)
            sent(core_sem.at[offset + 2 * far], partner)


def gather_blocks(own, count):
    levels = count // 4
    dma = pltpu.SemaphoreType.DMA
    return pl.pallas_call(
        functools.partial(gather_kernel, levels),
        out_shape=jax.ShapeDtypeStruct((count,) + own.shape, own.dtype),
        in_specs=[pl.BlockSpec(memory_space=pl.ANY)],
        out_specs=pl.BlockSpec(memory_space=pl.ANY),
        scratch_shapes=[
            dma,
            dma((levels,)),
            dma((levels,)),
            dma((2 * levels - 1,)),
            dma((2 * (2 * levels - 1),)),
            dma((count,)),
        ],
        compiler_params=pltpu.CompilerParams(collective_id=0, has_side_effects=True),
        cost_estimate=pl.CostEstimate(flops=7 * 10**10, bytes_accessed=count * own.size * 2, transcendentals=0),
    )(own)


def front_kernel(
    levels,
    tokens_ref,
    gain_ref,
    cos_ref,
    sin_ref,
    table_ref,
    start_ref,
    mlp_gain_ref,
    weight_ref,
    out_weight_ref,
    gate_up_ref,
    down_ref,
    rows_ref,
    residual_ref,
    key_ref,
    value_ref,
    slices_ref,
    pieces_ref,
    query_ref,
    out_columns,
    bias,
    attended,
    mine,
    theirs,
    got,
    arriving,
    staged,
    pair_columns,
    query_columns,
    normed,
    load_sem,
    keep_sem,
    token_sem,
    up_sem,
    down_sem,
    side_sem,
    core_sem,
    recv_sem,
    spread_sem,
    near_sem,
    pass_sem,
    over_sem,
    twin_sem,
    part_sem,
    rows_sem,
):
    count = 4 * levels
    me = lax.axis_index("seq")
    row = lax.axis_index("head")
    core = me % 2
    side = (me // 2) % 2
    level = me // 4
    has_above = level < levels - 1
    has_below = level > 0
    up = me + 4
    down = me - 4
    across = me + 2 - 4 * side
    partner = me + 1 - 2 * core
    height = tokens_ref.shape[0]
    groups = pair_columns.shape[0]
    heads = query_columns.shape[2] // HEAD_WIDTH
    span = (heads + 2) * HEAD_WIDTH
    width = slices_ref.shape[4]
    hidden_here = down_ref.shape[1]
    model = tokens_ref.shape[1]
    window = table_ref.shape[0]
    block = 2 * height

    def slot(at_level, at_side, at_core):
        return at_level * 4 + at_side * 2 + at_core

    def rows_of(half):
        return pl.ds(pl.multiple_of(half * height, height), height)

    def part(index, half):
        return pieces_ref.at[index, :, :, rows_of(half), :]

    def along(source, target_ref, send, recv, target):
        return pltpu.make_async_remote_copy(
            src_ref=source,
            dst_ref=target_ref,
            send_sem=send,
            recv_sem=recv,
            device_id={"seq": target},
            device_id_type=pl.DeviceIdType.MESH,
        )

    def over(source, target_ref, send, recv):
        return pltpu.make_async_remote_copy(
            src_ref=source,
            dst_ref=target_ref,
            send_sem=send,
            recv_sem=recv,
            device_id={"head": 1 - row},
            device_id_type=pl.DeviceIdType.MESH,
        )

    loads = []
    for group in range(groups):
        loads.append(
            pltpu.make_async_copy(
                weight_ref.at[:, pl.ds(group * span + heads * HEAD_WIDTH, 2 * HEAD_WIDTH)],
                pair_columns.at[group],
                load_sem.at[group],
            )
        )
    for group in range(groups):
        loads.append(
            pltpu.make_async_copy(
                weight_ref.at[:, pl.ds(group * span, heads * HEAD_WIDTH)],
                query_columns.at[group],
                load_sem.at[groups + group],
            )
        )
    loads.append(
        pltpu.make_async_copy(out_weight_ref, out_columns, load_sem.at[2 * groups])
    )
    for load in loads:
        load.start()

    barrier = pltpu.get_barrier_semaphore()

    @pl.loop(1, count)
    def _(step):
        pl.semaphore_signal(
            barrier,
            inc=1,
            device_id={"seq": (me + step) % count},
            device_id_type=pl.DeviceIdType.MESH,
        )

    pl.semaphore_signal(
        barrier, inc=1, device_id={"head": 1 - row}, device_id_type=pl.DeviceIdType.MESH
    )
    pl.semaphore_wait(barrier, count)

    token_copy = over(tokens_ref, arriving, token_sem.at[0], token_sem.at[1])
    token_copy.start()

    def slice_of(kind, target):
        first = (target % GROUP) * width
        if kind == 2:
            return down_ref.at[:, pl.ds(pl.multiple_of(first, width), width)]
        return gate_up_ref.at[:, pl.ds(pl.multiple_of(kind * hidden_here + first, width), width)]

    def own_slice(kind):
        return pltpu.make_async_copy(
            slice_of(kind, me), slices_ref.at[kind, 0, me], near_sem.at[kind, me]
        )

    def near(kind, source, step, target):
        return along(
            slice_of(kind, target),
            slices_ref.at[kind, 0, source],
            spread_sem.at[kind, step],
            near_sem.at[kind, source],
            target,
        )

    def cross(kind, source):
        return over(
            slices_ref.at[kind, 0, source],
            slices_ref.at[kind, 2, source],
            pass_sem.at[kind, source],
            over_sem.at[kind, source],
        )

    def twin(kind, which):
        return along(
            slices_ref.at[kind, 2 * which],
            slices_ref.at[kind, 2 * which + 1],
            twin_sem.at[kind, which, 0],
            twin_sem.at[kind, which, 1],
            partner,
        )

    def spread_out(kind):
        own_slice(kind).start()

        @pl.loop(1, count)
        def _(step):
            near(kind, me, step, (me + step) % count).start()

    def cross_over(kind):
        own_slice(kind).wait()
        cross(kind, me).start()

        @pl.loop(1, count)
        def _(step):
            source = (me + count - step) % count
            near(kind, source, step, partner).wait_recv()
            cross(kind, source).start()

        twin(kind, 0).start()

    def cross_twin(kind):
        @pl.loop(0, count)
        def _(source):
            cross(kind, source).wait_recv()

        twin(kind, 1).start()

    def settle(kind):
        @pl.loop(1, count)
        def _(step):
            near(kind, me, step, partner).wait_send()

        @pl.loop(0, count)
        def _(source):
            cross(kind, source).wait_send()

        twin(kind, 0).wait()
        twin(kind, 1).wait()

    spread_out(0)

    def norm(source):
        wide = source[...].astype(jnp.float32)
        factor = lax.rsqrt(jnp.mean(wide * wide, axis=-1, keepdims=True) + EPSILON)
        normed[...] = (wide * factor * gain_ref[...]).astype(jnp.bfloat16)

    def turned(values, number):
        return (
            values * cos_ref[number] + pltpu.roll(values, HEAD_WIDTH // 2, 1) * sin_ref[number]
        ).astype(jnp.bfloat16)

    def project_pairs(number, half):
        for group in range(groups):
            if number == 0:
                loads[group].wait()
            pair = jnp.dot(normed[...], pair_columns[group], preferred_element_type=jnp.float32)
            key = turned(pair[:, :HEAD_WIDTH], number)
            value = pair[:, HEAD_WIDTH:].astype(jnp.bfloat16)
            staged[number, 0, group] = key
            staged[number, 1, group] = value
            key_ref[group, rows_of(half), :] = key
            value_ref[group, rows_of(half), :] = value

    def project_queries(number, half):
        for group in range(groups):
            if number == 0:
                loads[groups + group].wait()
            found = jnp.dot(normed[...], query_columns[group], preferred_element_type=jnp.float32)
            for head in range(heads):
                first = pl.multiple_of(head * 2 * height + half * height, height)
                query_ref[group, pl.ds(first, height), :] = turned(
                    found[:, head * HEAD_WIDTH : (head + 1) * HEAD_WIDTH], number
                )

    last = 2 * levels - 1

    def copy(source, index, number, half, send, target):
        return along(source, part(index, half), send, recv_sem.at[number, index], target)

    def arrived(index, number, half):
        copy(part(index, half), index, number, half, keep_sem.at[number], partner).wait_recv()

    def keep(number, half):
        return pltpu.make_async_copy(staged.at[number], part(me, half), keep_sem.at[number])

    def send_own(number, half):
        source = staged.at[number]
        pl.when(has_above)(
            lambda: copy(source, me, number, half, up_sem.at[number, 0], up).start()
        )
        pl.when(has_below)(
            lambda: copy(source, me, number, half, down_sem.at[number, 0], down).start()
        )
        copy(source, me, number, half, side_sem.at[number, 0], across).start()
        copy(source, me, number, half, core_sem.at[number, 0], partner).start()
        keep(number, half).start()

    def forward(number, half):
        for far in range(1, levels):

            @pl.when(level - far >= 0)
            def _():
                index = slot(level - far, side, core)
                arrived(index, number, half)
                block = part(index, half)
                pl.when(has_above)(
                    lambda: copy(block, index, number, half, up_sem.at[number, far], up).start()
                )
                copy(block, index, number, half, side_sem.at[number, 2 * far - 1], across).start()
                copy(block, index, number, half, core_sem.at[number, 2 * far - 1], partner).start()

            @pl.when(level + far < levels)
            def _():
                index = slot(level + far, side, core)
                arrived(index, number, half)
                block = part(index, half)
                pl.when(has_below)(
                    lambda: copy(block, index, number, half, down_sem.at[number, far], down).start()
                )
                copy(block, index, number, half, side_sem.at[number, 2 * far], across).start()
                copy(block, index, number, half, core_sem.at[number, 2 * far], partner).start()

    def pass_on(at_level, number, half, place):
        index = slot(at_level, 1 - side, core)
        arrived(index, number, half)
        copy(
            part(index, half), index, number, half, core_sem.at[number, last + place], partner
        ).start()

    def pass_all(number, half):
        pass_on(level, number, half, 0)
        for far in range(1, levels):
            pl.when(level - far >= 0)(lambda: pass_on(level - far, number, half, 2 * far - 1))
            pl.when(level + far < levels)(lambda: pass_on(level + far, number, half, 2 * far))

    def finish(number, half):
        for at_level in range(levels):
            for at_side in range(2):
                arrived(slot(at_level, at_side, 1 - core), number, half)
        keep(number, half).wait()
        source = staged.at[number]

        def sent(sem, target):
            copy(source, me, number, half, sem, target).wait_send()

        pl.when(has_above)(lambda: sent(up_sem.at[number, 0], up))
        pl.when(has_below)(lambda: sent(down_sem.at[number, 0], down))
        sent(side_sem.at[number, 0], across)
        sent(core_sem.at[number, 0], partner)
        sent(core_sem.at[number, last], partner)
        for far in range(1, levels):

            @pl.when(level - far >= 0)
            def _():
                pl.when(has_above)(lambda: sent(up_sem.at[number, far], up))
                sent(side_sem.at[number, 2 * far - 1], across)
                sent(core_sem.at[number, 2 * far - 1], partner)
                sent(core_sem.at[number, last + 2 * far - 1], partner)

            @pl.when(level + far < levels)
            def _():
                pl.when(has_below)(lambda: sent(down_sem.at[number, far], down))
                sent(side_sem.at[number, 2 * far], across)
                sent(core_sem.at[number, 2 * far], partner)
                sent(core_sem.at[number, last + 2 * far], partner)

    def attend_group(group):
        keys = jnp.concatenate(
            [pieces_ref[table_ref[back], 0, group] for back in range(window)], axis=0
        )
        values = jnp.concatenate(
            [pieces_ref[table_ref[back], 1, group] for back in range(window)], axis=0
        )
        for head in range(heads):
            query = query_ref[group, head * block : (head + 1) * block, :]
            scores = lax.dot_general(
                query, keys, (((1,), (1,)), ((), ())), preferred_element_type=jnp.float32
            )
            scores = scores * (1.0 / math.sqrt(HEAD_WIDTH)) + bias[...]
            weights = jnp.exp(scores - jnp.max(scores, axis=1, keepdims=True))
            total = jnp.sum(weights, axis=1, keepdims=True)
            mixed = jnp.dot(
                weights.astype(jnp.bfloat16), values, preferred_element_type=jnp.float32
            )
            first = (group * heads + head) * HEAD_WIDTH
            attended[:, first : first + HEAD_WIDTH] = (mixed / total).astype(jnp.bfloat16)

    pieces_out = theirs.shape[0]
    out_width = model // pieces_out

    def swap(number):
        return over(
            theirs.at[number], got.at[number], part_sem.at[0, number], part_sem.at[1, number]
        )

    def gathered(source, target_ref, number, target):
        return along(source, target_ref, rows_sem.at[0, number], rows_sem.at[1, number], target)

    half_rows = height // 2
    low = pl.ds(0, half_rows)
    high = pl.ds(half_rows, half_rows)
    climb = me + 4 - 8 * (level % 2)
    to_side = gathered(rows_ref.at[0], rows_ref.at[1], 0, across)
    to_level = gathered(rows_ref.at[0], rows_ref.at[2], 1, climb)
    side_to_level = gathered(rows_ref.at[1, low], rows_ref.at[3, low], 2, climb)
    level_to_side = gathered(rows_ref.at[2, high], rows_ref.at[3, high], 3, across)

    norm(tokens_ref)
    project_pairs(0, row)
    send_own(0, row)
    project_queries(0, row)
    token_copy.wait_recv()
    norm(arriving)
    project_pairs(1, 1 - row)
    send_own(1, 1 - row)
    project_queries(1, 1 - row)
    forward(0, row)
    cross_over(0)
    forward(1, 1 - row)
    pass_all(0, row)
    pass_all(1, 1 - row)
    spread_out(1)
    column = lax.broadcasted_iota(jnp.int32, bias.shape, 1)
    line = lax.broadcasted_iota(jnp.int32, bias.shape, 0)
    visible = (column >= start_ref[...]) & (column <= line + (window - 1) * block)
    bias[...] = jnp.where(visible, 0.0, -1e30)
    token_copy.wait_send()
    finish(0, row)
    finish(1, 1 - row)
    cross_twin(0)
    spread_out(2)
    for group in range(groups):
        attend_group(group)
    cross_over(1)
    loads[2 * groups].wait()
    for number in range(pieces_out):
        columns = slice(number * out_width, (number + 1) * out_width)
        theirs[number] = jnp.dot(
            attended[rows_of(1 - row), :],
            out_columns[:, columns],
            preferred_element_type=jnp.float32,
        ).astype(jnp.bfloat16)
        swap(number).start()
    for number in range(pieces_out):
        columns = slice(number * out_width, (number + 1) * out_width)
        mine[:, columns] = jnp.dot(
            attended[rows_of(row), :], out_columns[:, columns], preferred_element_type=jnp.float32
        )
    cross_over(2)
    for number in range(pieces_out):
        columns = slice(number * out_width, (number + 1) * out_width)
        swap(number).wait()
        total = tokens_ref[:, columns].astype(jnp.float32) + (
            mine[:, columns] + got[number].astype(jnp.float32)
        )
        residual_ref[:, columns] = total.astype(jnp.bfloat16)
    wide = residual_ref[...].astype(jnp.float32)
    factor = lax.rsqrt(jnp.mean(wide * wide, axis=-1, keepdims=True) + EPSILON)
    rows_ref[0] = (wide * factor * mlp_gain_ref[...]).astype(jnp.bfloat16)
    to_side.start()
    to_level.start()
    cross_twin(1)
    to_side.wait_recv()
    side_to_level.start()
    to_level.wait_recv()
    level_to_side.start()
    cross_twin(2)
    side_to_level.wait()
    level_to_side.wait()
    to_side.wait_send()
    to_level.wait_send()
    for kind in range(3):
        settle(kind)


PIECES_OUT = 2


def front(tokens, gain, cosine, sine, table, starts, mlp_gain, weight, out_weight, gate_up_rows, down_rows, blocks):
    levels = blocks // 4
    height, model = tokens.shape
    heads = QUERY_HEAD_COUNT // KEY_VALUE_HEADS
    groups = weight.shape[1] // ((heads + 2) * HEAD_WIDTH)
    width = down_rows.shape[1] // GROUP
    window = table.shape[0]
    dma = pltpu.SemaphoreType.DMA
    anywhere = pl.BlockSpec(memory_space=pl.ANY)
    vmem = pl.BlockSpec(memory_space=pltpu.VMEM)
    kind = jnp.bfloat16
    return pl.pallas_call(
        functools.partial(front_kernel, levels),
        out_shape=[
            jax.ShapeDtypeStruct((4, height, model), kind),
            jax.ShapeDtypeStruct((height, model), kind),
            jax.ShapeDtypeStruct((groups, 2 * height, HEAD_WIDTH), kind),
            jax.ShapeDtypeStruct((groups, 2 * height, HEAD_WIDTH), kind),
            jax.ShapeDtypeStruct((3, 4, blocks, down_rows.shape[0], width), kind),
        ],
        in_specs=[vmem] * 4
        + [pl.BlockSpec(memory_space=pltpu.SMEM)]
        + [vmem] * 2
        + [anywhere] * 4,
        out_specs=[vmem, vmem, vmem, vmem, anywhere],
        scratch_shapes=[
            pltpu.VMEM((blocks, 2, groups, 2 * height, HEAD_WIDTH), kind),
            pltpu.VMEM((groups, heads * 2 * height, HEAD_WIDTH), kind),
            pltpu.VMEM(out_weight.shape, kind),
            pltpu.VMEM((2 * height, window * 2 * height), jnp.float32),
            pltpu.VMEM((2 * height, out_weight.shape[0]), kind),
            pltpu.VMEM((height, model), jnp.float32),
            pltpu.VMEM((PIECES_OUT, height, model // PIECES_OUT), kind),
            pltpu.VMEM((PIECES_OUT, height, model // PIECES_OUT), kind),
            pltpu.VMEM((height, model), kind),
            pltpu.VMEM((2, 2, groups, height, HEAD_WIDTH), kind),
            pltpu.VMEM((groups, model, 2 * HEAD_WIDTH), kind),
            pltpu.VMEM((groups, model, heads * HEAD_WIDTH), kind),
            pltpu.VMEM((height, model), kind),
            dma((2 * groups + 1,)),
            dma((2,)),
            dma((2,)),
            dma((2, levels)),
            dma((2, levels)),
            dma((2, 2 * levels - 1)),
            dma((2, 2 * (2 * levels - 1))),
            dma((2, blocks)),
            dma((3, blocks)),
            dma((3, blocks)),
            dma((3, blocks)),
            dma((3, blocks)),
            dma((3, 2, 2)),
            dma((2, PIECES_OUT)),
            dma((2, 4)),
        ],
        compiler_params=pltpu.CompilerParams(
            collective_id=1, has_side_effects=True, vmem_limit_bytes=60 * 1024 * 1024
        ),
        cost_estimate=pl.CostEstimate(
            flops=7 * 10**10, bytes_accessed=weight.size * 2, transcendentals=0
        ),
    )(tokens, gain, cosine, sine, table, starts, mlp_gain, weight, out_weight, gate_up_rows, down_rows)


def attention_kernel(window, table_ref, start_ref, query_ref, *refs):
    keys = refs[:window]
    values = refs[window : 2 * window]
    out_ref = refs[2 * window]
    block = keys[0].shape[-2]
    query = query_ref[0]
    heads = query.shape[0] // block
    local = jnp.concatenate([start_ref[...]] * heads, axis=0)
    row = lax.broadcasted_iota(jnp.int32, (block, 1), 0)
    row = jnp.concatenate([row] * heads, axis=0)
    key_all = jnp.concatenate([ref[0, 0, 0] for ref in keys], axis=0)
    value_all = jnp.concatenate([ref[0, 0, 0] for ref in values], axis=0)
    scores = lax.dot_general(
        query, key_all, (((1,), (1,)), ((), ())), preferred_element_type=jnp.float32
    ) * (1.0 / math.sqrt(HEAD_WIDTH))
    column = lax.broadcasted_iota(jnp.int32, scores.shape, 1)
    visible = (column >= local) & (column <= row + (window - 1) * block)
    masked = jnp.where(visible, scores, -1e30)
    top = jnp.max(masked, axis=1, keepdims=True)
    weights = jnp.exp(masked - top)
    total = jnp.sum(weights, axis=1, keepdims=True)
    mixed = jnp.dot(weights.astype(jnp.bfloat16), value_all, preferred_element_type=jnp.float32)
    out_ref[0] = (mixed / total).astype(jnp.bfloat16)


def attend(query_heads, pieces, table, local_starts, window):
    groups, rows, width = query_heads.shape
    block = local_starts.shape[0]

    def spec(kind, back):
        return pl.BlockSpec(
            (1, 1, 1, block, width),
            lambda g, table_ref: (table_ref[back], kind, g, 0, 0),
        )

    flops = 4 * groups * rows * window * block * width
    return pl.pallas_call(
        functools.partial(attention_kernel, window),
        grid_spec=pltpu.PrefetchScalarGridSpec(
            num_scalar_prefetch=1,
            grid=(groups,),
            in_specs=[
                pl.BlockSpec((block, 1), lambda g, *_: (0, 0)),
                pl.BlockSpec((1, rows, width), lambda g, *_: (g, 0, 0)),
            ]
            + [spec(0, back) for back in range(window)]
            + [spec(1, back) for back in range(window)],
            out_specs=pl.BlockSpec((1, rows, width), lambda g, *_: (g, 0, 0)),
        ),
        out_shape=jax.ShapeDtypeStruct(query_heads.shape, jnp.bfloat16),
        compiler_params=pltpu.CompilerParams(vmem_limit_bytes=48 * 1024 * 1024),
        cost_estimate=pl.CostEstimate(
            flops=flops,
            bytes_accessed=groups * (rows * 2 + window * block * 2) * width * 2,
            transcendentals=groups * rows * window * block,
        ),
    )(table, local_starts, query_heads, *([pieces] * (2 * window)))


def exchange(values, axis, flip):
    count = lax.axis_size(axis)
    return lax.ppermute(values, axis, [(i, i ^ flip) for i in range(count)])


TILE = 512


def mlp_kernel(rows_ref, slices_ref, out_ref, gates, ups, downs, hidden, sem):
    copies = []
    for kind, kept in enumerate((gates, ups, downs)):
        copies.append(
            [
                pltpu.make_async_copy(
                    slices_ref.at[kind, piece], kept.at[piece], sem.at[4 * kind + piece]
                )
                for piece in range(4)
            ]
        )
    for piece in range(4):
        copies[0][piece].start()
        copies[1][piece].start()
    for piece in range(4):
        copies[2][piece].start()
    for piece in range(4):
        copies[0][piece].wait()
        gate = jnp.dot(rows_ref[...], gates[piece], preferred_element_type=jnp.float32)
        copies[1][piece].wait()
        up = jnp.dot(rows_ref[...], ups[piece], preferred_element_type=jnp.float32)
        hidden[piece] = (gate / (1.0 + jnp.exp(-gate)) * up).astype(jnp.bfloat16)
    for piece in range(4):
        copies[2][piece].wait()

    @pl.loop(0, out_ref.shape[1] // TILE)
    def _(tile):
        first = pl.multiple_of(tile * TILE, TILE)
        total = None
        for piece in range(4):
            term = down_product(hidden[piece], downs[piece, pl.ds(first, TILE), :])
            total = term if total is None else total + term
        out_ref[:, pl.ds(first, TILE)] = total.astype(jnp.bfloat16)


def mlp(blocks, slices):
    model = blocks.shape[2]
    width = slices.shape[3]
    rows = 4 * blocks.shape[1]
    return pl.pallas_call(
        mlp_kernel,
        in_specs=[pl.BlockSpec(memory_space=pltpu.VMEM), pl.BlockSpec(memory_space=pl.ANY)],
        out_specs=pl.BlockSpec(memory_space=pltpu.VMEM),
        out_shape=jax.ShapeDtypeStruct((rows, model), jnp.bfloat16),
        scratch_shapes=[
            pltpu.VMEM((4, model, width), jnp.bfloat16),
            pltpu.VMEM((4, model, width), jnp.bfloat16),
            pltpu.VMEM((4, model, width), jnp.bfloat16),
            pltpu.VMEM((4, rows, width), jnp.bfloat16),
            pltpu.SemaphoreType.DMA((12,)),
        ],
        compiler_params=pltpu.CompilerParams(vmem_limit_bytes=48 * 1024 * 1024),
        cost_estimate=pl.CostEstimate(
            flops=2 * rows * model * width * 12,
            bytes_accessed=12 * model * width * 2 + 2 * rows * model * 2,
            transcendentals=rows * width * 4,
        ),
    )(blocks.reshape(rows, model), slices)


def combine(partial, residual):
    model = residual.shape[1]

    def wide(values):
        return values.astype(jnp.float32)

    results = []
    middle = model // 2
    for first, second, near, far, columns in (
        (SIDE, LEVEL, 1, 2, slice(0, middle)),
        (LEVEL, SIDE, 2, 1, slice(middle, model)),
    ):
        block = partial[:, :, columns]
        got = exchange(jnp.stack([block[near], block[3]]), "seq", first)
        passed = (wide(block[far]) + wide(got[1])).astype(jnp.bfloat16)
        last = exchange(passed, "seq", second)
        total = wide(residual[:, columns]) + (wide(block[0]) + wide(got[0]) + wide(last))
        results.append(total.astype(jnp.bfloat16))
    return jnp.concatenate(results, axis=1)


def grouped_layer(
    tokens, rope_pos, inverse, table, local_starts, window, attn_gain, query_key_value_weight,
    out_weight, mlp_gain, gate_up_weight, down_weight, head_index, blocks,
):
    rows_here = tokens.shape[0]
    hidden_here = gate_up_weight.shape[2]
    angles = rope_pos.astype(jnp.float32)[:, None] * inverse[None, :]
    cosine = jnp.cos(angles)
    sine = jnp.sin(angles)

    def own_first(values):
        halves = values.reshape(2, rows_here, HEAD_WIDTH)
        return jnp.where(head_index == 0, halves, halves[::-1])

    cosine = own_first(jnp.concatenate([cosine, cosine], axis=1))
    sine = own_first(jnp.concatenate([-sine, sine], axis=1))
    gate_up_rows = gate_up_weight.reshape(gate_up_weight.shape[0], 2 * hidden_here)
    rows, residual, key_cache, value_cache, slices = front(
        tokens, attn_gain[None, :], cosine, sine, table, local_starts, mlp_gain[None, :],
        query_key_value_weight, out_weight, gate_up_rows, down_weight, blocks,
    )
    model = tokens.shape[1]
    partial = mlp(rows, slices.reshape(3, 4, model, slices.shape[4]))
    output = combine(partial.reshape(4, rows_here, model), residual)
    return (output, key_cache, value_cache)


def shards(
    tokens,
    segment_ids,
    lengths,
    deal,
    attn_gain,
    query_key_value_weight,
    out_weight,
    mlp_gain,
    gate_up_weight,
    down_weight,
):
    head_count = lax.axis_size("head")
    head_index = lax.axis_index("head")
    seq_index = lax.axis_index("seq")
    rows_here = tokens.shape[0]
    block_rows = rows_here * head_count
    heads_per_group = QUERY_HEAD_COUNT // KEY_VALUE_HEADS
    groups = query_key_value_weight.shape[1] // ((heads_per_group + 2) * HEAD_WIDTH)
    blocks = deal.shape[0]
    longest = segment_ids.shape[0] // 4
    window = min(blocks, -(-(longest - 1) // block_rows) + 1)
    hidden_here = gate_up_weight.shape[2]
    grouped = head_count == 2 and blocks % GROUP == 0 and hidden_here % (GROUP * 128) == 0
    if not grouped:
        weight_rows = jnp.concatenate(
            [gate_up_weight.reshape(gate_up_weight.shape[0], 2 * hidden_here), down_weight], axis=1
        )
        weights_all = lax.all_gather(weight_rows, "seq", axis=0, tiled=True)
    block_ids = jnp.arange(blocks, dtype=jnp.int32)
    my_block = jnp.sum(jnp.where(block_ids == seq_index, deal, 0))
    stream_pos = my_block * block_rows + jnp.arange(block_rows, dtype=jnp.int32)
    query_segments = lax.dynamic_slice_in_dim(segment_ids, my_block * block_rows, block_rows, 0)
    prompts = jnp.arange(lengths.shape[0], dtype=jnp.int32)
    starts = jnp.sum(jnp.where(prompts[None, :] < prompts[:, None], lengths[None, :], 0), axis=1)
    prompt_hits = query_segments[:, None] == jnp.arange(lengths.shape[0], dtype=jnp.int32)[None, :]
    query_starts = jnp.sum(jnp.where(prompt_hits, starts[None, :], 0), axis=1)
    rope_pos = stream_pos - query_starts
    wanted = jnp.maximum(my_block - (window - 1) + jnp.arange(window, dtype=jnp.int32), 0)
    table = jnp.sum(
        jnp.where(wanted[:, None] == deal[None, :], block_ids[None, :], 0), axis=1
    ).astype(jnp.int32)
    local_starts = (query_starts - (my_block - (window - 1)) * block_rows)[:, None]
    inverse = frequencies(HEAD_WIDTH)
    if grouped:
        return grouped_layer(
            tokens, rope_pos, inverse, table, local_starts, window, attn_gain, query_key_value_weight,
            out_weight, mlp_gain, gate_up_weight, down_weight, head_index, blocks,
        )
    full_rows = jnp.zeros((block_rows, tokens.shape[1]), tokens.dtype)
    full_rows = lax.dynamic_update_slice_in_dim(full_rows, tokens, head_index * rows_here, 0)
    for step in range(1, head_count):
        source = (head_index - step) % head_count
        full_rows = lax.dynamic_update_slice_in_dim(
            full_rows, shift(tokens, step, head_count), source * rows_here, 0
        )
    projected_rows = jnp.dot(
        normalize(full_rows, attn_gain), query_key_value_weight, preferred_element_type=jnp.float32
    )
    projected_rows = projected_rows.reshape(block_rows, groups, heads_per_group + 2, HEAD_WIDTH)
    queries = rotate(projected_rows[:, :, :heads_per_group], rope_pos, inverse).astype(jnp.bfloat16)
    key_matrix = rotate(
        projected_rows[:, :, heads_per_group : heads_per_group + 1], rope_pos, inverse
    )[:, :, 0].astype(jnp.bfloat16)
    value_matrix = projected_rows[:, :, heads_per_group + 1].astype(jnp.bfloat16)
    key_cache = jnp.transpose(key_matrix, (1, 0, 2))
    value_cache = jnp.transpose(value_matrix, (1, 0, 2))
    query_heads = jnp.transpose(queries, (1, 2, 0, 3)).reshape(
        groups, heads_per_group * block_rows, HEAD_WIDTH
    )
    key_value = jnp.stack([key_cache, value_cache])
    pieces = gather_blocks(key_value, blocks)
    attended = attend(query_heads, pieces, table, local_starts, window)
    attended = jnp.transpose(
        attended.reshape(groups, heads_per_group, block_rows, HEAD_WIDTH), (2, 0, 1, 3)
    ).reshape(block_rows, groups * heads_per_group * HEAD_WIDTH)
    part = jnp.dot(attended, out_weight, preferred_element_type=jnp.float32).astype(jnp.bfloat16)
    total_proj = part.astype(jnp.float32)
    for step in range(1, head_count):
        total_proj = total_proj + shift(part, step, head_count).astype(jnp.float32)
    full_residual = (full_rows.astype(jnp.float32) + total_proj).astype(jnp.bfloat16)
    mlp_in = lax.optimization_barrier(normalize(full_residual, mlp_gain))
    residual = lax.dynamic_slice_in_dim(full_residual, head_index * rows_here, rows_here, 0)
    gate = jnp.dot(mlp_in, weights_all[:, :hidden_here], preferred_element_type=jnp.float32)
    up = jnp.dot(
        mlp_in, weights_all[:, hidden_here : 2 * hidden_here], preferred_element_type=jnp.float32
    )
    hidden = (jax.nn.silu(gate) * up).astype(jnp.bfloat16)
    chunks = []
    pieces_down = 3
    width = weights_all.shape[0] // pieces_down
    for number in range(pieces_down):
        columns = slice(number * width, (number + 1) * width)
        terms = down_product(hidden, weights_all[columns, 2 * hidden_here :]).astype(jnp.bfloat16)
        total = residual[:, columns].astype(jnp.float32) + lax.dynamic_slice_in_dim(
            terms, head_index * rows_here, rows_here, 0
        ).astype(jnp.float32)
        for step in range(1, head_count):
            target = (head_index + step) % head_count
            piece = lax.dynamic_slice_in_dim(terms, target * rows_here, rows_here, 0)
            total = total + shift(piece, step, head_count).astype(jnp.float32)
        chunks.append(total.astype(jnp.bfloat16))
    output = jnp.concatenate(chunks, axis=1)
    return (output, key_cache, value_cache)


def solution(mesh):
    placed = (
        P(("seq", "head"), None),
        P(),
        P(),
        P(),
        P(),
        P(None, "head"),
        P("head", None),
        P(),
        P("seq", None, "head"),
        P("seq", "head"),
    )
    return jax.shard_map(
        shards,
        mesh=mesh,
        in_specs=placed,
        out_specs=(P(("seq", "head"), None), P("head", "seq", None), P("head", "seq", None)),
        check_vma=False,
    )
```

```python
import functools
import math

import jax
import jax.numpy as jnp
from jax import lax
from jax.experimental import pallas as pl
from jax.experimental.pallas import tpu as pltpu
from jax.sharding import PartitionSpec as P

QUERY_HEAD_COUNT = 24
KEY_VALUE_HEADS = 8
HEAD_WIDTH = 128


EPSILON = 1e-05
CORE = 1
SIDE = 2
LEVEL = 4
GROUP = 8
ROPE_BASE = 500000.0


def frequencies(head_size):
    exponent = jnp.arange(0, head_size, 2, dtype=jnp.float32) / head_size
    inverse = 1.0 / ROPE_BASE**exponent
    wavelength = 2.0 * math.pi / inverse
    smooth = (8192.0 / wavelength - 1.0) / 3.0
    blended = (1.0 - smooth) * inverse / 32.0 + smooth * inverse
    return jnp.where(
        wavelength > 8192.0, inverse / 32.0, jnp.where(wavelength < 2048.0, inverse, blended)
    )


def rotate(row_values, position, inverse):
    angles = position.astype(jnp.float32)[:, None] * inverse[None, :]
    cosine = jnp.cos(angles)[:, None, None, :]
    sine_term = jnp.sin(angles)[:, None, None, :]
    half_size = row_values.shape[-1] // 2
    first_half = row_values[..., :half_size]
    second_half = row_values[..., half_size:]
    return jnp.concatenate(
        [
            first_half * cosine - second_half * sine_term,
            second_half * cosine + first_half * sine_term,
        ],
        axis=-1,
    )


def normalize(row_values, gain_vector):
    values_wide = row_values.astype(jnp.float32)
    factor = lax.rsqrt(jnp.mean(values_wide * values_wide, axis=-1, keepdims=True) + EPSILON)
    return (values_wide * factor * gain_vector).astype(jnp.bfloat16)


def down_product(hidden, down_rows):
    return lax.dot_general(
        hidden, down_rows, (((1,), (1,)), ((), ())), preferred_element_type=jnp.float32
    )


def shift(values, step, count):
    return lax.ppermute(values, "head", [(i, (i + step) % count) for i in range(count)])


def gather_kernel(levels, own_ref, out_ref, copy_sem, up_sem, down_sem, side_sem, core_sem, recv_sem):
    me = lax.axis_index("seq")
    core = me % 2
    side = (me // 2) % 2
    level = me // 4
    has_above = level < levels - 1
    has_below = level > 0

    def slot(at_level, at_side, at_core):
        return at_level * 4 + at_side * 2 + at_core

    up = me + 4
    down = me - 4
    across = me + 2 - 4 * side
    partner = me + 1 - 2 * core

    def copy(source, index, send_sem, target):
        return pltpu.make_async_remote_copy(
            src_ref=source,
            dst_ref=out_ref.at[index],
            send_sem=send_sem,
            recv_sem=recv_sem.at[index],
            device_id={"seq": target},
            device_id_type=pl.DeviceIdType.MESH,
        )

    def arrived(index):
        copy(out_ref.at[index], index, copy_sem, partner).wait_recv()

    def greet(target):
        pl.semaphore_signal(
            barrier, inc=1, device_id={"seq": target}, device_id_type=pl.DeviceIdType.MESH
        )

    barrier = pltpu.get_barrier_semaphore()
    greet(partner)
    greet(across)
    pl.when(has_above)(lambda: greet(up))
    pl.when(has_below)(lambda: greet(down))
    peers = 2 + jnp.where(has_above, 1, 0) + jnp.where(has_below, 1, 0)
    pl.semaphore_wait(barrier, peers)

    pl.when(has_above)(lambda: copy(own_ref, me, up_sem.at[0], up).start())
    pl.when(has_below)(lambda: copy(own_ref, me, down_sem.at[0], down).start())
    copy(own_ref, me, side_sem.at[0], across).start()
    copy(own_ref, me, core_sem.at[0], partner).start()
    keep = pltpu.make_async_copy(own_ref, out_ref.at[me], copy_sem)
    keep.start()

    for far in range(1, levels):

        @pl.when(level - far >= 0)
        def _():
            index = slot(level - far, side, core)
            arrived(index)
            block = out_ref.at[index]
            pl.when(has_above)(lambda: copy(block, index, up_sem.at[far], up).start())
            copy(block, index, side_sem.at[2 * far - 1], across).start()
            copy(block, index, core_sem.at[2 * far - 1], partner).start()

        @pl.when(level + far < levels)
        def _():
            index = slot(level + far, side, core)
            arrived(index)
            block = out_ref.at[index]
            pl.when(has_below)(lambda: copy(block, index, down_sem.at[far], down).start())
            copy(block, index, side_sem.at[2 * far], across).start()
            copy(block, index, core_sem.at[2 * far], partner).start()

    offset = 2 * levels - 1

    def pass_on(at_level, number):
        index = slot(at_level, 1 - side, core)
        arrived(index)
        copy(out_ref.at[index], index, core_sem.at[offset + number], partner).start()

    pass_on(level, 0)
    for far in range(1, levels):
        pl.when(level - far >= 0)(lambda: pass_on(level - far, 2 * far - 1))
        pl.when(level + far < levels)(lambda: pass_on(level + far, 2 * far))

    for at_level in range(levels):
        for at_side in range(2):
            arrived(slot(at_level, at_side, 1 - core))

    keep.wait()

    def sent(sem, target):
        copy(own_ref, me, sem, target).wait_send()

    pl.when(has_above)(lambda: sent(up_sem.at[0], up))
    pl.when(has_below)(lambda: sent(down_sem.at[0], down))
    sent(side_sem.at[0], across)
    sent(core_sem.at[0], partner)
    sent(core_sem.at[offset], partner)
    for far in range(1, levels):

        @pl.when(level - far >= 0)
        def _():
            pl.when(has_above)(lambda: sent(up_sem.at[far], up))
            sent(side_sem.at[2 * far - 1], across)
            sent(core_sem.at[2 * far - 1], partner)
            sent(core_sem.at[offset + 2 * far - 1], partner)

        @pl.when(level + far < levels)
        def _():
            pl.when(has_below)(lambda: sent(down_sem.at[far], down))
            sent(side_sem.at[2 * far], across)
            sent(core_sem.at[2 * far], partner)
            sent(core_sem.at[offset + 2 * far], partner)


def gather_blocks(own, count):
    levels = count // 4
    dma = pltpu.SemaphoreType.DMA
    return pl.pallas_call(
        functools.partial(gather_kernel, levels),
        out_shape=jax.ShapeDtypeStruct((count,) + own.shape, own.dtype),
        in_specs=[pl.BlockSpec(memory_space=pl.ANY)],
        out_specs=pl.BlockSpec(memory_space=pl.ANY),
        scratch_shapes=[
            dma,
            dma((levels,)),
            dma((levels,)),
            dma((2 * levels - 1,)),
            dma((2 * (2 * levels - 1),)),
            dma((count,)),
        ],
        compiler_params=pltpu.CompilerParams(collective_id=0, has_side_effects=True),
        cost_estimate=pl.CostEstimate(flops=7 * 10**10, bytes_accessed=count * own.size * 2, transcendentals=0),
    )(own)


def front_kernel(
    levels,
    tokens_ref,
    gain_ref,
    cos_ref,
    sin_ref,
    table_ref,
    start_ref,
    mlp_gain_ref,
    weight_ref,
    out_weight_ref,
    gate_up_ref,
    down_ref,
    rows_ref,
    residual_ref,
    key_ref,
    value_ref,
    slices_ref,
    pieces_ref,
    query_ref,
    out_columns,
    bias,
    attended,
    mine,
    theirs,
    got,
    arriving,
    staged,
    pair_columns,
    query_columns,
    normed,
    load_sem,
    keep_sem,
    token_sem,
    up_sem,
    down_sem,
    side_sem,
    core_sem,
    recv_sem,
    spread_sem,
    near_sem,
    pass_sem,
    over_sem,
    twin_sem,
    part_sem,
    rows_sem,
):
    count = 4 * levels
    me = lax.axis_index("seq")
    row = lax.axis_index("head")
    core = me % 2
    side = (me // 2) % 2
    level = me // 4
    has_above = level < levels - 1
    has_below = level > 0
    up = me + 4
    down = me - 4
    across = me + 2 - 4 * side
    partner = me + 1 - 2 * core
    height = tokens_ref.shape[0]
    groups = pair_columns.shape[0]
    heads = query_columns.shape[2] // HEAD_WIDTH
    span = (heads + 2) * HEAD_WIDTH
    width = slices_ref.shape[4]
    hidden_here = down_ref.shape[1]
    model = tokens_ref.shape[1]
    window = table_ref.shape[0]
    block = 2 * height

    def slot(at_level, at_side, at_core):
        return at_level * 4 + at_side * 2 + at_core

    def rows_of(half):
        return pl.ds(pl.multiple_of(half * height, height), height)

    def part(index, half):
        return pieces_ref.at[index, :, :, rows_of(half), :]

    def along(source, target_ref, send, recv, target):
        return pltpu.make_async_remote_copy(
            src_ref=source,
            dst_ref=target_ref,
            send_sem=send,
            recv_sem=recv,
            device_id={"seq": target},
            device_id_type=pl.DeviceIdType.MESH,
        )

    def over(source, target_ref, send, recv):
        return pltpu.make_async_remote_copy(
            src_ref=source,
            dst_ref=target_ref,
            send_sem=send,
            recv_sem=recv,
            device_id={"head": 1 - row},
            device_id_type=pl.DeviceIdType.MESH,
        )

    loads = []
    for group in range(groups):
        loads.append(
            pltpu.make_async_copy(
                weight_ref.at[:, pl.ds(group * span + heads * HEAD_WIDTH, 2 * HEAD_WIDTH)],
                pair_columns.at[group],
                load_sem.at[group],
            )
        )
    for group in range(groups):
        loads.append(
            pltpu.make_async_copy(
                weight_ref.at[:, pl.ds(group * span, heads * HEAD_WIDTH)],
                query_columns.at[group],
                load_sem.at[groups + group],
            )
        )
    loads.append(
        pltpu.make_async_copy(out_weight_ref, out_columns, load_sem.at[2 * groups])
    )
    for load in loads:
        load.start()

    barrier = pltpu.get_barrier_semaphore()

    @pl.loop(1, count)
    def _(step):
        pl.semaphore_signal(
            barrier,
            inc=1,
            device_id={"seq": (me + step) % count},
            device_id_type=pl.DeviceIdType.MESH,
        )

    pl.semaphore_signal(
        barrier, inc=1, device_id={"head": 1 - row}, device_id_type=pl.DeviceIdType.MESH
    )
    pl.semaphore_wait(barrier, count)

    token_copy = over(tokens_ref, arriving, token_sem.at[0], token_sem.at[1])
    token_copy.start()

    def slice_of(kind, target):
        first = (target % GROUP) * width
        if kind == 2:
            return down_ref.at[:, pl.ds(pl.multiple_of(first, width), width)]
        return gate_up_ref.at[:, pl.ds(pl.multiple_of(kind * hidden_here + first, width), width)]

    def own_slice(kind):
        return pltpu.make_async_copy(
            slice_of(kind, me), slices_ref.at[kind, 0, me], near_sem.at[kind, me]
        )

    def near(kind, source, step, target):
        return along(
            slice_of(kind, target),
            slices_ref.at[kind, 0, source],
            spread_sem.at[kind, step],
            near_sem.at[kind, source],
            target,
        )

    def cross(kind, source):
        return over(
            slices_ref.at[kind, 0, source],
            slices_ref.at[kind, 2, source],
            pass_sem.at[kind, source],
            over_sem.at[kind, source],
        )

    def twin(kind, which):
        return along(
            slices_ref.at[kind, 2 * which],
            slices_ref.at[kind, 2 * which + 1],
            twin_sem.at[kind, which, 0],
            twin_sem.at[kind, which, 1],
            partner,
        )

    place = me % GROUP
    family = me // GROUP
    families = count // GROUP

    def toward(step):
        return ((family + step // GROUP) % families) * GROUP + (place + step) % GROUP

    def away(step):
        return ((family + families - step // GROUP) % families) * GROUP + (
            place + GROUP - step % GROUP
        ) % GROUP

    def spread_steps(kind, first, end):
        @pl.loop(first, end)
        def _(step):
            near(kind, me, step, toward(step)).start()

    def spread_own(kind):
        own_slice(kind).start()
        spread_steps(kind, 1, GROUP)

    def spread_far(kind):
        spread_steps(kind, GROUP, count)

    def cross_steps(kind, first, end):
        @pl.loop(first, end)
        def _(step):
            source = away(step)
            near(kind, source, step, partner).wait_recv()
            cross(kind, source).start()

    def cross_own(kind):
        own_slice(kind).wait()
        cross(kind, me).start()
        cross_steps(kind, 1, GROUP)

    def cross_far(kind):
        cross_steps(kind, GROUP, count)
        twin(kind, 0).start()

    def cross_twin(kind):
        @pl.loop(0, count)
        def _(source):
            cross(kind, source).wait_recv()

        twin(kind, 1).start()

    def settle(kind):
        @pl.loop(1, count)
        def _(step):
            near(kind, me, step, partner).wait_send()

        @pl.loop(0, count)
        def _(source):
            cross(kind, source).wait_send()

        twin(kind, 0).wait()
        twin(kind, 1).wait()

    spread_own(0)
    spread_own(1)
    spread_own(2)
    def norm(source):
        wide = source[...].astype(jnp.float32)
        factor = lax.rsqrt(jnp.mean(wide * wide, axis=-1, keepdims=True) + EPSILON)
        normed[...] = (wide * factor * gain_ref[...]).astype(jnp.bfloat16)

    def turned(values, number):
        return (
            values * cos_ref[number] + pltpu.roll(values, HEAD_WIDTH // 2, 1) * sin_ref[number]
        ).astype(jnp.bfloat16)

    def project_pairs(number, half):
        for group in range(groups):
            if number == 0:
                loads[group].wait()
            pair = jnp.dot(normed[...], pair_columns[group], preferred_element_type=jnp.float32)
            key = turned(pair[:, :HEAD_WIDTH], number)
            value = pair[:, HEAD_WIDTH:].astype(jnp.bfloat16)
            staged[number, 0, group] = key
            staged[number, 1, group] = value
            key_ref[group, rows_of(half), :] = key
            value_ref[group, rows_of(half), :] = value

    def project_queries(number, half):
        for group in range(groups):
            if number == 0:
                loads[groups + group].wait()
            found = jnp.dot(normed[...], query_columns[group], preferred_element_type=jnp.float32)
            for head in range(heads):
                first = pl.multiple_of(head * 2 * height + half * height, height)
                query_ref[group, pl.ds(first, height), :] = turned(
                    found[:, head * HEAD_WIDTH : (head + 1) * HEAD_WIDTH], number
                )

    last = 2 * levels - 1

    def copy(source, index, number, half, send, target):
        return along(source, part(index, half), send, recv_sem.at[number, index], target)

    def arrived(index, number, half):
        copy(part(index, half), index, number, half, keep_sem.at[number], partner).wait_recv()

    def keep(number, half):
        return pltpu.make_async_copy(staged.at[number], part(me, half), keep_sem.at[number])

    def send_own(number, half):
        source = staged.at[number]
        pl.when(has_above)(
            lambda: copy(source, me, number, half, up_sem.at[number, 0], up).start()
        )
        pl.when(has_below)(
            lambda: copy(source, me, number, half, down_sem.at[number, 0], down).start()
        )
        copy(source, me, number, half, side_sem.at[number, 0], across).start()
        copy(source, me, number, half, core_sem.at[number, 0], partner).start()
        keep(number, half).start()

    def forward(number, half):
        for far in range(1, levels):

            @pl.when(level - far >= 0)
            def _():
                index = slot(level - far, side, core)
                arrived(index, number, half)
                block = part(index, half)
                pl.when(has_above)(
                    lambda: copy(block, index, number, half, up_sem.at[number, far], up).start()
                )
                copy(block, index, number, half, side_sem.at[number, 2 * far - 1], across).start()
                copy(block, index, number, half, core_sem.at[number, 2 * far - 1], partner).start()

            @pl.when(level + far < levels)
            def _():
                index = slot(level + far, side, core)
                arrived(index, number, half)
                block = part(index, half)
                pl.when(has_below)(
                    lambda: copy(block, index, number, half, down_sem.at[number, far], down).start()
                )
                copy(block, index, number, half, side_sem.at[number, 2 * far], across).start()
                copy(block, index, number, half, core_sem.at[number, 2 * far], partner).start()

    def pass_on(at_level, number, half, place):
        index = slot(at_level, 1 - side, core)
        arrived(index, number, half)
        copy(
            part(index, half), index, number, half, core_sem.at[number, last + place], partner
        ).start()

    def pass_all(number, half):
        pass_on(level, number, half, 0)
        for far in range(1, levels):
            pl.when(level - far >= 0)(lambda: pass_on(level - far, number, half, 2 * far - 1))
            pl.when(level + far < levels)(lambda: pass_on(level + far, number, half, 2 * far))

    def finish(number, half):
        for at_level in range(levels):
            for at_side in range(2):
                arrived(slot(at_level, at_side, 1 - core), number, half)
        keep(number, half).wait()
        source = staged.at[number]

        def sent(sem, target):
            copy(source, me, number, half, sem, target).wait_send()

        pl.when(has_above)(lambda: sent(up_sem.at[number, 0], up))
        pl.when(has_below)(lambda: sent(down_sem.at[number, 0], down))
        sent(side_sem.at[number, 0], across)
        sent(core_sem.at[number, 0], partner)
        sent(core_sem.at[number, last], partner)
        for far in range(1, levels):

            @pl.when(level - far >= 0)
            def _():
                pl.when(has_above)(lambda: sent(up_sem.at[number, far], up))
                sent(side_sem.at[number, 2 * far - 1], across)
                sent(core_sem.at[number, 2 * far - 1], partner)
                sent(core_sem.at[number, last + 2 * far - 1], partner)

            @pl.when(level + far < levels)
            def _():
                pl.when(has_below)(lambda: sent(down_sem.at[number, far], down))
                sent(side_sem.at[number, 2 * far], across)
                sent(core_sem.at[number, 2 * far], partner)
                sent(core_sem.at[number, last + 2 * far], partner)

    def attend_group(group):
        keys = jnp.concatenate(
            [pieces_ref[table_ref[back], 0, group] for back in range(window)], axis=0
        )
        values = jnp.concatenate(
            [pieces_ref[table_ref[back], 1, group] for back in range(window)], axis=0
        )
        for head in range(heads):
            query = query_ref[group, head * block : (head + 1) * block, :]
            scores = lax.dot_general(
                query, keys, (((1,), (1,)), ((), ())), preferred_element_type=jnp.float32
            )
            scores = scores * (1.0 / math.sqrt(HEAD_WIDTH)) + bias[...]
            weights = jnp.exp(scores - jnp.max(scores, axis=1, keepdims=True))
            total = jnp.sum(weights, axis=1, keepdims=True)
            mixed = jnp.dot(
                weights.astype(jnp.bfloat16), values, preferred_element_type=jnp.float32
            )
            first = (group * heads + head) * HEAD_WIDTH
            attended[:, first : first + HEAD_WIDTH] = (mixed / total).astype(jnp.bfloat16)

    pieces_out = theirs.shape[0]
    out_width = model // pieces_out

    def swap(number):
        return over(
            theirs.at[number], got.at[number], part_sem.at[0, number], part_sem.at[1, number]
        )

    def gathered(source, target_ref, number, target):
        return along(source, target_ref, rows_sem.at[0, number], rows_sem.at[1, number], target)

    half_rows = height // 2
    low = pl.ds(0, half_rows)
    high = pl.ds(half_rows, half_rows)
    climb = me + 4 - 8 * (level % 2)
    to_side = gathered(rows_ref.at[0], rows_ref.at[1], 0, across)
    to_level = gathered(rows_ref.at[0], rows_ref.at[3], 1, climb)
    side_to_level = gathered(rows_ref.at[1, low], rows_ref.at[2, low], 2, climb)
    level_to_side = gathered(rows_ref.at[3, high], rows_ref.at[2, high], 3, across)

    norm(tokens_ref)
    project_pairs(0, row)
    send_own(0, row)
    project_queries(0, row)
    token_copy.wait_recv()
    norm(arriving)
    project_pairs(1, 1 - row)
    send_own(1, 1 - row)
    project_queries(1, 1 - row)
    cross_own(0)
    cross_own(1)
    cross_own(2)
    forward(0, row)
    spread_far(0)
    forward(1, 1 - row)
    spread_far(1)
    pass_all(0, row)
    pass_all(1, 1 - row)
    cross_far(0)
    column = lax.broadcasted_iota(jnp.int32, bias.shape, 1)
    line = lax.broadcasted_iota(jnp.int32, bias.shape, 0)
    visible = (column >= start_ref[...]) & (column <= line + (window - 1) * block)
    bias[...] = jnp.where(visible, 0.0, -1e30)
    token_copy.wait_send()
    finish(0, row)
    finish(1, 1 - row)
    spread_far(2)
    for group in range(groups):
        attend_group(group)
    loads[2 * groups].wait()
    for number in range(pieces_out):
        columns = slice(number * out_width, (number + 1) * out_width)
        theirs[number] = jnp.dot(
            attended[rows_of(1 - row), :],
            out_columns[:, columns],
            preferred_element_type=jnp.float32,
        ).astype(jnp.bfloat16)
        swap(number).start()
    for number in range(pieces_out):
        columns = slice(number * out_width, (number + 1) * out_width)
        mine[:, columns] = jnp.dot(
            attended[rows_of(row), :], out_columns[:, columns], preferred_element_type=jnp.float32
        )
    cross_far(1)
    cross_twin(0)
    for number in range(pieces_out):
        columns = slice(number * out_width, (number + 1) * out_width)
        swap(number).wait()
        total = tokens_ref[:, columns].astype(jnp.float32) + (
            mine[:, columns] + got[number].astype(jnp.float32)
        )
        residual_ref[:, columns] = total.astype(jnp.bfloat16)
    wide = residual_ref[...].astype(jnp.float32)
    factor = lax.rsqrt(jnp.mean(wide * wide, axis=-1, keepdims=True) + EPSILON)
    rows_ref[0] = (wide * factor * mlp_gain_ref[...]).astype(jnp.bfloat16)
    to_side.start()
    to_level.start()
    cross_far(2)
    cross_twin(1)
    to_side.wait_recv()
    side_to_level.start()
    to_level.wait_recv()
    level_to_side.start()
    cross_twin(2)
    side_to_level.wait()
    level_to_side.wait()
    to_side.wait_send()
    to_level.wait_send()
    for kind in range(3):
        settle(kind)


PIECES_OUT = 2


def front(tokens, gain, cosine, sine, table, starts, mlp_gain, weight, out_weight, gate_up_rows, down_rows, blocks):
    levels = blocks // 4
    height, model = tokens.shape
    heads = QUERY_HEAD_COUNT // KEY_VALUE_HEADS
    groups = weight.shape[1] // ((heads + 2) * HEAD_WIDTH)
    width = down_rows.shape[1] // GROUP
    window = table.shape[0]
    dma = pltpu.SemaphoreType.DMA
    anywhere = pl.BlockSpec(memory_space=pl.ANY)
    vmem = pl.BlockSpec(memory_space=pltpu.VMEM)
    kind = jnp.bfloat16
    return pl.pallas_call(
        functools.partial(front_kernel, levels),
        out_shape=[
            jax.ShapeDtypeStruct((4, height, model), kind),
            jax.ShapeDtypeStruct((height, model), kind),
            jax.ShapeDtypeStruct((groups, 2 * height, HEAD_WIDTH), kind),
            jax.ShapeDtypeStruct((groups, 2 * height, HEAD_WIDTH), kind),
            jax.ShapeDtypeStruct((3, 4, blocks, down_rows.shape[0], width), kind),
        ],
        in_specs=[vmem] * 4
        + [pl.BlockSpec(memory_space=pltpu.SMEM)]
        + [vmem] * 2
        + [anywhere] * 4,
        out_specs=[vmem, vmem, vmem, vmem, anywhere],
        scratch_shapes=[
            pltpu.VMEM((blocks, 2, groups, 2 * height, HEAD_WIDTH), kind),
            pltpu.VMEM((groups, heads * 2 * height, HEAD_WIDTH), kind),
            pltpu.VMEM(out_weight.shape, kind),
            pltpu.VMEM((2 * height, window * 2 * height), jnp.float32),
            pltpu.VMEM((2 * height, out_weight.shape[0]), kind),
            pltpu.VMEM((height, model), jnp.float32),
            pltpu.VMEM((PIECES_OUT, height, model // PIECES_OUT), kind),
            pltpu.VMEM((PIECES_OUT, height, model // PIECES_OUT), kind),
            pltpu.VMEM((height, model), kind),
            pltpu.VMEM((2, 2, groups, height, HEAD_WIDTH), kind),
            pltpu.VMEM((groups, model, 2 * HEAD_WIDTH), kind),
            pltpu.VMEM((groups, model, heads * HEAD_WIDTH), kind),
            pltpu.VMEM((height, model), kind),
            dma((2 * groups + 1,)),
            dma((2,)),
            dma((2,)),
            dma((2, levels)),
            dma((2, levels)),
            dma((2, 2 * levels - 1)),
            dma((2, 2 * (2 * levels - 1))),
            dma((2, blocks)),
            dma((3, blocks)),
            dma((3, blocks)),
            dma((3, blocks)),
            dma((3, blocks)),
            dma((3, 2, 2)),
            dma((2, PIECES_OUT)),
            dma((2, 4)),
        ],
        compiler_params=pltpu.CompilerParams(
            collective_id=1, has_side_effects=True, vmem_limit_bytes=60 * 1024 * 1024
        ),
        cost_estimate=pl.CostEstimate(
            flops=7 * 10**10, bytes_accessed=weight.size * 2, transcendentals=0
        ),
    )(tokens, gain, cosine, sine, table, starts, mlp_gain, weight, out_weight, gate_up_rows, down_rows)


def attention_kernel(window, table_ref, start_ref, query_ref, *refs):
    keys = refs[:window]
    values = refs[window : 2 * window]
    out_ref = refs[2 * window]
    block = keys[0].shape[-2]
    query = query_ref[0]
    heads = query.shape[0] // block
    local = jnp.concatenate([start_ref[...]] * heads, axis=0)
    row = lax.broadcasted_iota(jnp.int32, (block, 1), 0)
    row = jnp.concatenate([row] * heads, axis=0)
    key_all = jnp.concatenate([ref[0, 0, 0] for ref in keys], axis=0)
    value_all = jnp.concatenate([ref[0, 0, 0] for ref in values], axis=0)
    scores = lax.dot_general(
        query, key_all, (((1,), (1,)), ((), ())), preferred_element_type=jnp.float32
    ) * (1.0 / math.sqrt(HEAD_WIDTH))
    column = lax.broadcasted_iota(jnp.int32, scores.shape, 1)
    visible = (column >= local) & (column <= row + (window - 1) * block)
    masked = jnp.where(visible, scores, -1e30)
    top = jnp.max(masked, axis=1, keepdims=True)
    weights = jnp.exp(masked - top)
    total = jnp.sum(weights, axis=1, keepdims=True)
    mixed = jnp.dot(weights.astype(jnp.bfloat16), value_all, preferred_element_type=jnp.float32)
    out_ref[0] = (mixed / total).astype(jnp.bfloat16)


def attend(query_heads, pieces, table, local_starts, window):
    groups, rows, width = query_heads.shape
    block = local_starts.shape[0]

    def spec(kind, back):
        return pl.BlockSpec(
            (1, 1, 1, block, width),
            lambda g, table_ref: (table_ref[back], kind, g, 0, 0),
        )

    flops = 4 * groups * rows * window * block * width
    return pl.pallas_call(
        functools.partial(attention_kernel, window),
        grid_spec=pltpu.PrefetchScalarGridSpec(
            num_scalar_prefetch=1,
            grid=(groups,),
            in_specs=[
                pl.BlockSpec((block, 1), lambda g, *_: (0, 0)),
                pl.BlockSpec((1, rows, width), lambda g, *_: (g, 0, 0)),
            ]
            + [spec(0, back) for back in range(window)]
            + [spec(1, back) for back in range(window)],
            out_specs=pl.BlockSpec((1, rows, width), lambda g, *_: (g, 0, 0)),
        ),
        out_shape=jax.ShapeDtypeStruct(query_heads.shape, jnp.bfloat16),
        compiler_params=pltpu.CompilerParams(vmem_limit_bytes=48 * 1024 * 1024),
        cost_estimate=pl.CostEstimate(
            flops=flops,
            bytes_accessed=groups * (rows * 2 + window * block * 2) * width * 2,
            transcendentals=groups * rows * window * block,
        ),
    )(table, local_starts, query_heads, *([pieces] * (2 * window)))


TILE = 256


CHUNKS = 4


def mlp_kernel(
    rows_ref, residual_ref, slices_ref, out_ref, gates, ups, downs, hidden, held, first_in, second_in, sem, sum_sem
):
    me = lax.axis_index("seq")
    across = me + 2 - 4 * ((me // 2) % 2)
    climb = me + 4 - 8 * ((me // 4) % 2)
    height = residual_ref.shape[0]
    model = residual_ref.shape[1]
    chunk_width = model // CHUNKS
    copies = []
    for kind, kept in enumerate((gates, ups, downs)):
        copies.append(
            [
                pltpu.make_async_copy(
                    slices_ref.at[kind, piece], kept.at[piece], sem.at[4 * kind + piece]
                )
                for piece in range(4)
            ]
        )
    for piece in range(4):
        copies[0][piece].start()
        copies[1][piece].start()
    for piece in range(4):
        copies[2][piece].start()
    barrier = pltpu.get_barrier_semaphore()
    for target in (across, climb):
        pl.semaphore_signal(
            barrier, inc=1, device_id={"seq": target}, device_id_type=pl.DeviceIdType.MESH
        )
    for piece in range(4):
        copies[0][piece].wait()
        gate = jnp.dot(rows_ref[...], gates[piece], preferred_element_type=jnp.float32)
        copies[1][piece].wait()
        up = jnp.dot(rows_ref[...], ups[piece], preferred_element_type=jnp.float32)
        hidden[piece] = (gate / (1.0 + jnp.exp(-gate)) * up).astype(jnp.bfloat16)
    for piece in range(4):
        copies[2][piece].wait()
    pl.semaphore_wait(barrier, 2)

    def along(source, target_ref, number, target):
        return pltpu.make_async_remote_copy(
            src_ref=source,
            dst_ref=target_ref,
            send_sem=sum_sem.at[0, number],
            recv_sem=sum_sem.at[1, number],
            device_id={"seq": target},
            device_id_type=pl.DeviceIdType.MESH,
        )

    def columns_of(chunk):
        return pl.ds(chunk * chunk_width, chunk_width)

    def block(number):
        return pl.ds(number * height, height)

    def first_hop(chunk):
        start, target = (1, across) if chunk % 2 == 0 else (2, climb)
        return along(
            held.at[pl.ds(start * height, 2 * height), columns_of(chunk)],
            first_in.at[:, columns_of(chunk)],
            chunk,
            target,
        )

    def second_hop(chunk):
        start, target = (3, climb) if chunk % 2 == 0 else (1, across)
        return along(
            held.at[block(start), columns_of(chunk)],
            second_in.at[:, columns_of(chunk)],
            CHUNKS + chunk,
            target,
        )

    def wide(ref, rows, chunk):
        return ref[rows, columns_of(chunk)].astype(jnp.float32)

    for chunk in range(CHUNKS):

        @pl.loop(0, chunk_width // TILE)
        def _(tile):
            first = pl.multiple_of(chunk * chunk_width + tile * TILE, TILE)
            total = None
            for piece in range(4):
                term = down_product(hidden[piece], downs[piece, pl.ds(first, TILE), :])
                total = term if total is None else total + term
            held[:, pl.ds(first, TILE)] = total.astype(jnp.bfloat16)

        first_hop(chunk).start()
    for chunk in range(CHUNKS):
        first_hop(chunk).wait_recv()
        passing = 3 if chunk % 2 == 0 else 1
        total = wide(held, block(passing), chunk) + wide(first_in, block(1 - chunk % 2), chunk)
        held[block(passing), columns_of(chunk)] = total.astype(jnp.bfloat16)
        second_hop(chunk).start()
    for chunk in range(CHUNKS):
        columns = columns_of(chunk)
        total = (
            residual_ref[:, columns].astype(jnp.float32)
            + wide(held, block(0), chunk)
            + wide(first_in, block(chunk % 2), chunk)
        )
        second_hop(chunk).wait_recv()
        out_ref[:, columns] = (total + second_in[:, columns].astype(jnp.float32)).astype(
            jnp.bfloat16
        )
    for chunk in range(CHUNKS):
        first_hop(chunk).wait_send()
        second_hop(chunk).wait_send()


def mlp(blocks, residual, slices):
    model = blocks.shape[2]
    width = slices.shape[3]
    height = residual.shape[0]
    rows = 4 * height
    vmem = pl.BlockSpec(memory_space=pltpu.VMEM)
    kind = jnp.bfloat16
    return pl.pallas_call(
        mlp_kernel,
        in_specs=[vmem, vmem, pl.BlockSpec(memory_space=pl.ANY)],
        out_specs=vmem,
        out_shape=jax.ShapeDtypeStruct((height, model), kind),
        scratch_shapes=[
            pltpu.VMEM((4, model, width), kind),
            pltpu.VMEM((4, model, width), kind),
            pltpu.VMEM((4, model, width), kind),
            pltpu.VMEM((4, rows, width), kind),
            pltpu.VMEM((rows, model), kind),
            pltpu.VMEM((2 * height, model), kind),
            pltpu.VMEM((height, model), kind),
            pltpu.SemaphoreType.DMA((12,)),
            pltpu.SemaphoreType.DMA((2, 2 * CHUNKS)),
        ],
        compiler_params=pltpu.CompilerParams(
            collective_id=2, has_side_effects=True, vmem_limit_bytes=48 * 1024 * 1024
        ),
        cost_estimate=pl.CostEstimate(
            flops=2 * rows * model * width * 12,
            bytes_accessed=12 * model * width * 2 + 2 * rows * model * 2,
            transcendentals=rows * width * 4,
        ),
    )(blocks.reshape(rows, model), residual, slices)


def grouped_layer(
    tokens, rope_pos, inverse, table, local_starts, window, attn_gain, query_key_value_weight,
    out_weight, mlp_gain, gate_up_weight, down_weight, head_index, blocks,
):
    rows_here = tokens.shape[0]
    hidden_here = gate_up_weight.shape[2]
    angles = rope_pos.astype(jnp.float32)[:, None] * inverse[None, :]
    cosine = jnp.cos(angles)
    sine = jnp.sin(angles)

    def own_first(values):
        halves = values.reshape(2, rows_here, HEAD_WIDTH)
        return jnp.where(head_index == 0, halves, halves[::-1])

    cosine = own_first(jnp.concatenate([cosine, cosine], axis=1))
    sine = own_first(jnp.concatenate([-sine, sine], axis=1))
    gate_up_rows = gate_up_weight.reshape(gate_up_weight.shape[0], 2 * hidden_here)
    rows, residual, key_cache, value_cache, slices = front(
        tokens, attn_gain[None, :], cosine, sine, table, local_starts, mlp_gain[None, :],
        query_key_value_weight, out_weight, gate_up_rows, down_weight, blocks,
    )
    model = tokens.shape[1]
    output = mlp(rows, residual, slices.reshape(3, 4, model, slices.shape[4]))
    return (output, key_cache, value_cache)


def shards(
    tokens,
    segment_ids,
    lengths,
    deal,
    attn_gain,
    query_key_value_weight,
    out_weight,
    mlp_gain,
    gate_up_weight,
    down_weight,
):
    head_count = lax.axis_size("head")
    head_index = lax.axis_index("head")
    seq_index = lax.axis_index("seq")
    rows_here = tokens.shape[0]
    block_rows = rows_here * head_count
    heads_per_group = QUERY_HEAD_COUNT // KEY_VALUE_HEADS
    groups = query_key_value_weight.shape[1] // ((heads_per_group + 2) * HEAD_WIDTH)
    blocks = deal.shape[0]
    longest = segment_ids.shape[0] // 4
    window = min(blocks, -(-(longest - 1) // block_rows) + 1)
    hidden_here = gate_up_weight.shape[2]
    grouped = head_count == 2 and blocks % GROUP == 0 and hidden_here % (GROUP * 128) == 0
    if not grouped:
        weight_rows = jnp.concatenate(
            [gate_up_weight.reshape(gate_up_weight.shape[0], 2 * hidden_here), down_weight], axis=1
        )
        weights_all = lax.all_gather(weight_rows, "seq", axis=0, tiled=True)
    block_ids = jnp.arange(blocks, dtype=jnp.int32)
    my_block = jnp.sum(jnp.where(block_ids == seq_index, deal, 0))
    stream_pos = my_block * block_rows + jnp.arange(block_rows, dtype=jnp.int32)
    query_segments = lax.dynamic_slice_in_dim(segment_ids, my_block * block_rows, block_rows, 0)
    prompts = jnp.arange(lengths.shape[0], dtype=jnp.int32)
    starts = jnp.sum(jnp.where(prompts[None, :] < prompts[:, None], lengths[None, :], 0), axis=1)
    prompt_hits = query_segments[:, None] == jnp.arange(lengths.shape[0], dtype=jnp.int32)[None, :]
    query_starts = jnp.sum(jnp.where(prompt_hits, starts[None, :], 0), axis=1)
    rope_pos = stream_pos - query_starts
    wanted = jnp.maximum(my_block - (window - 1) + jnp.arange(window, dtype=jnp.int32), 0)
    table = jnp.sum(
        jnp.where(wanted[:, None] == deal[None, :], block_ids[None, :], 0), axis=1
    ).astype(jnp.int32)
    local_starts = (query_starts - (my_block - (window - 1)) * block_rows)[:, None]
    inverse = frequencies(HEAD_WIDTH)
    if grouped:
        return grouped_layer(
            tokens, rope_pos, inverse, table, local_starts, window, attn_gain, query_key_value_weight,
            out_weight, mlp_gain, gate_up_weight, down_weight, head_index, blocks,
        )
    full_rows = jnp.zeros((block_rows, tokens.shape[1]), tokens.dtype)
    full_rows = lax.dynamic_update_slice_in_dim(full_rows, tokens, head_index * rows_here, 0)
    for step in range(1, head_count):
        source = (head_index - step) % head_count
        full_rows = lax.dynamic_update_slice_in_dim(
            full_rows, shift(tokens, step, head_count), source * rows_here, 0
        )
    projected_rows = jnp.dot(
        normalize(full_rows, attn_gain), query_key_value_weight, preferred_element_type=jnp.float32
    )
    projected_rows = projected_rows.reshape(block_rows, groups, heads_per_group + 2, HEAD_WIDTH)
    queries = rotate(projected_rows[:, :, :heads_per_group], rope_pos, inverse).astype(jnp.bfloat16)
    key_matrix = rotate(
        projected_rows[:, :, heads_per_group : heads_per_group + 1], rope_pos, inverse
    )[:, :, 0].astype(jnp.bfloat16)
    value_matrix = projected_rows[:, :, heads_per_group + 1].astype(jnp.bfloat16)
    key_cache = jnp.transpose(key_matrix, (1, 0, 2))
    value_cache = jnp.transpose(value_matrix, (1, 0, 2))
    query_heads = jnp.transpose(queries, (1, 2, 0, 3)).reshape(
        groups, heads_per_group * block_rows, HEAD_WIDTH
    )
    key_value = jnp.stack([key_cache, value_cache])
    pieces = gather_blocks(key_value, blocks)
    attended = attend(query_heads, pieces, table, local_starts, window)
    attended = jnp.transpose(
        attended.reshape(groups, heads_per_group, block_rows, HEAD_WIDTH), (2, 0, 1, 3)
    ).reshape(block_rows, groups * heads_per_group * HEAD_WIDTH)
    part = jnp.dot(attended, out_weight, preferred_element_type=jnp.float32).astype(jnp.bfloat16)
    total_proj = part.astype(jnp.float32)
    for step in range(1, head_count):
        total_proj = total_proj + shift(part, step, head_count).astype(jnp.float32)
    full_residual = (full_rows.astype(jnp.float32) + total_proj).astype(jnp.bfloat16)
    mlp_in = lax.optimization_barrier(normalize(full_residual, mlp_gain))
    residual = lax.dynamic_slice_in_dim(full_residual, head_index * rows_here, rows_here, 0)
    gate = jnp.dot(mlp_in, weights_all[:, :hidden_here], preferred_element_type=jnp.float32)
    up = jnp.dot(
        mlp_in, weights_all[:, hidden_here : 2 * hidden_here], preferred_element_type=jnp.float32
    )
    hidden = (jax.nn.silu(gate) * up).astype(jnp.bfloat16)
    chunks = []
    pieces_down = 3
    width = weights_all.shape[0] // pieces_down
    for number in range(pieces_down):
        columns = slice(number * width, (number + 1) * width)
        terms = down_product(hidden, weights_all[columns, 2 * hidden_here :]).astype(jnp.bfloat16)
        total = residual[:, columns].astype(jnp.float32) + lax.dynamic_slice_in_dim(
            terms, head_index * rows_here, rows_here, 0
        ).astype(jnp.float32)
        for step in range(1, head_count):
            target = (head_index + step) % head_count
            piece = lax.dynamic_slice_in_dim(terms, target * rows_here, rows_here, 0)
            total = total + shift(piece, step, head_count).astype(jnp.float32)
        chunks.append(total.astype(jnp.bfloat16))
    output = jnp.concatenate(chunks, axis=1)
    return (output, key_cache, value_cache)


def solution(mesh):
    placed = (
        P(("seq", "head"), None),
        P(),
        P(),
        P(),
        P(),
        P(None, "head"),
        P("head", None),
        P(),
        P("seq", None, "head"),
        P("seq", "head"),
    )
    return jax.shard_map(
        shards,
        mesh=mesh,
        in_specs=placed,
        out_specs=(P(("seq", "head"), None), P("head", "seq", None), P("head", "seq", None)),
        check_vma=False,
    )
```

```python
import functools
import math

import jax
import jax.numpy as jnp
from jax import lax
from jax.experimental import pallas as pl
from jax.experimental.pallas import tpu as pltpu
from jax.sharding import PartitionSpec as P

QUERY_HEAD_COUNT = 24
KEY_VALUE_HEADS = 8
HEAD_WIDTH = 128


EPSILON = 1e-05
CORE = 1
SIDE = 2
LEVEL = 4
GROUP = 8
ROPE_BASE = 500000.0


def frequencies(head_size):
    exponent = jnp.arange(0, head_size, 2, dtype=jnp.float32) / head_size
    inverse = 1.0 / ROPE_BASE**exponent
    wavelength = 2.0 * math.pi / inverse
    smooth = (8192.0 / wavelength - 1.0) / 3.0
    blended = (1.0 - smooth) * inverse / 32.0 + smooth * inverse
    return jnp.where(
        wavelength > 8192.0, inverse / 32.0, jnp.where(wavelength < 2048.0, inverse, blended)
    )


def rotate(row_values, position, inverse):
    angles = position.astype(jnp.float32)[:, None] * inverse[None, :]
    cosine = jnp.cos(angles)[:, None, None, :]
    sine_term = jnp.sin(angles)[:, None, None, :]
    half_size = row_values.shape[-1] // 2
    first_half = row_values[..., :half_size]
    second_half = row_values[..., half_size:]
    return jnp.concatenate(
        [
            first_half * cosine - second_half * sine_term,
            second_half * cosine + first_half * sine_term,
        ],
        axis=-1,
    )


def normalize(row_values, gain_vector):
    values_wide = row_values.astype(jnp.float32)
    factor = lax.rsqrt(jnp.mean(values_wide * values_wide, axis=-1, keepdims=True) + EPSILON)
    return (values_wide * factor * gain_vector).astype(jnp.bfloat16)


def down_product(hidden, down_rows):
    return lax.dot_general(
        hidden, down_rows, (((1,), (1,)), ((), ())), preferred_element_type=jnp.float32
    )


def shift(values, step, count):
    return lax.ppermute(values, "head", [(i, (i + step) % count) for i in range(count)])


def gather_kernel(levels, own_ref, out_ref, copy_sem, up_sem, down_sem, side_sem, core_sem, recv_sem):
    me = lax.axis_index("seq")
    core = me % 2
    side = (me // 2) % 2
    level = me // 4
    has_above = level < levels - 1
    has_below = level > 0

    def slot(at_level, at_side, at_core):
        return at_level * 4 + at_side * 2 + at_core

    up = me + 4
    down = me - 4
    across = me + 2 - 4 * side
    partner = me + 1 - 2 * core

    def copy(source, index, send_sem, target):
        return pltpu.make_async_remote_copy(
            src_ref=source,
            dst_ref=out_ref.at[index],
            send_sem=send_sem,
            recv_sem=recv_sem.at[index],
            device_id={"seq": target},
            device_id_type=pl.DeviceIdType.MESH,
        )

    def arrived(index):
        copy(out_ref.at[index], index, copy_sem, partner).wait_recv()

    def greet(target):
        pl.semaphore_signal(
            barrier, inc=1, device_id={"seq": target}, device_id_type=pl.DeviceIdType.MESH
        )

    barrier = pltpu.get_barrier_semaphore()
    greet(partner)
    greet(across)
    pl.when(has_above)(lambda: greet(up))
    pl.when(has_below)(lambda: greet(down))
    peers = 2 + jnp.where(has_above, 1, 0) + jnp.where(has_below, 1, 0)
    pl.semaphore_wait(barrier, peers)

    pl.when(has_above)(lambda: copy(own_ref, me, up_sem.at[0], up).start())
    pl.when(has_below)(lambda: copy(own_ref, me, down_sem.at[0], down).start())
    copy(own_ref, me, side_sem.at[0], across).start()
    copy(own_ref, me, core_sem.at[0], partner).start()
    keep = pltpu.make_async_copy(own_ref, out_ref.at[me], copy_sem)
    keep.start()

    for far in range(1, levels):

        @pl.when(level - far >= 0)
        def _():
            index = slot(level - far, side, core)
            arrived(index)
            block = out_ref.at[index]
            pl.when(has_above)(lambda: copy(block, index, up_sem.at[far], up).start())
            copy(block, index, side_sem.at[2 * far - 1], across).start()
            copy(block, index, core_sem.at[2 * far - 1], partner).start()

        @pl.when(level + far < levels)
        def _():
            index = slot(level + far, side, core)
            arrived(index)
            block = out_ref.at[index]
            pl.when(has_below)(lambda: copy(block, index, down_sem.at[far], down).start())
            copy(block, index, side_sem.at[2 * far], across).start()
            copy(block, index, core_sem.at[2 * far], partner).start()

    offset = 2 * levels - 1

    def pass_on(at_level, number):
        index = slot(at_level, 1 - side, core)
        arrived(index)
        copy(out_ref.at[index], index, core_sem.at[offset + number], partner).start()

    pass_on(level, 0)
    for far in range(1, levels):
        pl.when(level - far >= 0)(lambda: pass_on(level - far, 2 * far - 1))
        pl.when(level + far < levels)(lambda: pass_on(level + far, 2 * far))

    for at_level in range(levels):
        for at_side in range(2):
            arrived(slot(at_level, at_side, 1 - core))

    keep.wait()

    def sent(sem, target):
        copy(own_ref, me, sem, target).wait_send()

    pl.when(has_above)(lambda: sent(up_sem.at[0], up))
    pl.when(has_below)(lambda: sent(down_sem.at[0], down))
    sent(side_sem.at[0], across)
    sent(core_sem.at[0], partner)
    sent(core_sem.at[offset], partner)
    for far in range(1, levels):

        @pl.when(level - far >= 0)
        def _():
            pl.when(has_above)(lambda: sent(up_sem.at[far], up))
            sent(side_sem.at[2 * far - 1], across)
            sent(core_sem.at[2 * far - 1], partner)
            sent(core_sem.at[offset + 2 * far - 1], partner)

        @pl.when(level + far < levels)
        def _():
            pl.when(has_below)(lambda: sent(down_sem.at[far], down))
            sent(side_sem.at[2 * far], across)
            sent(core_sem.at[2 * far], partner)
            sent(core_sem.at[offset + 2 * far], partner)


def gather_blocks(own, count):
    levels = count // 4
    dma = pltpu.SemaphoreType.DMA
    return pl.pallas_call(
        functools.partial(gather_kernel, levels),
        out_shape=jax.ShapeDtypeStruct((count,) + own.shape, own.dtype),
        in_specs=[pl.BlockSpec(memory_space=pl.ANY)],
        out_specs=pl.BlockSpec(memory_space=pl.ANY),
        scratch_shapes=[
            dma,
            dma((levels,)),
            dma((levels,)),
            dma((2 * levels - 1,)),
            dma((2 * (2 * levels - 1),)),
            dma((count,)),
        ],
        compiler_params=pltpu.CompilerParams(collective_id=0, has_side_effects=True),
        cost_estimate=pl.CostEstimate(flops=7 * 10**10, bytes_accessed=count * own.size * 2, transcendentals=0),
    )(own)


def front_kernel(
    levels,
    tokens_ref,
    gain_ref,
    cos_ref,
    sin_ref,
    table_ref,
    start_ref,
    mlp_gain_ref,
    weight_ref,
    out_weight_ref,
    gate_up_ref,
    down_ref,
    rows_ref,
    residual_ref,
    key_ref,
    value_ref,
    slices_ref,
    pieces_ref,
    query_ref,
    out_columns,
    bias,
    attended,
    mine,
    theirs,
    got,
    arriving,
    staged,
    pair_columns,
    query_columns,
    normed,
    load_sem,
    keep_sem,
    token_sem,
    up_sem,
    down_sem,
    side_sem,
    core_sem,
    recv_sem,
    spread_sem,
    near_sem,
    pass_sem,
    over_sem,
    twin_sem,
    part_sem,
    rows_sem,
):
    count = 4 * levels
    me = lax.axis_index("seq")
    row = lax.axis_index("head")
    core = me % 2
    side = (me // 2) % 2
    level = me // 4
    has_above = level < levels - 1
    has_below = level > 0
    up = me + 4
    down = me - 4
    across = me + 2 - 4 * side
    partner = me + 1 - 2 * core
    height = tokens_ref.shape[0]
    groups = pair_columns.shape[0]
    heads = query_columns.shape[2] // HEAD_WIDTH
    span = (heads + 2) * HEAD_WIDTH
    width = slices_ref.shape[4]
    hidden_here = down_ref.shape[1]
    model = tokens_ref.shape[1]
    window = table_ref.shape[0]
    block = 2 * height

    def slot(at_level, at_side, at_core):
        return at_level * 4 + at_side * 2 + at_core

    def rows_of(half):
        return pl.ds(pl.multiple_of(half * height, height), height)

    def part(index, half):
        return pieces_ref.at[index, :, :, rows_of(half), :]

    def along(source, target_ref, send, recv, target):
        return pltpu.make_async_remote_copy(
            src_ref=source,
            dst_ref=target_ref,
            send_sem=send,
            recv_sem=recv,
            device_id={"seq": target},
            device_id_type=pl.DeviceIdType.MESH,
        )

    def over(source, target_ref, send, recv):
        return pltpu.make_async_remote_copy(
            src_ref=source,
            dst_ref=target_ref,
            send_sem=send,
            recv_sem=recv,
            device_id={"head": 1 - row},
            device_id_type=pl.DeviceIdType.MESH,
        )

    loads = []
    for group in range(groups):
        loads.append(
            pltpu.make_async_copy(
                weight_ref.at[:, pl.ds(group * span + heads * HEAD_WIDTH, 2 * HEAD_WIDTH)],
                pair_columns.at[group],
                load_sem.at[group],
            )
        )
    for group in range(groups):
        loads.append(
            pltpu.make_async_copy(
                weight_ref.at[:, pl.ds(group * span, heads * HEAD_WIDTH)],
                query_columns.at[group],
                load_sem.at[groups + group],
            )
        )
    loads.append(
        pltpu.make_async_copy(out_weight_ref, out_columns, load_sem.at[2 * groups])
    )
    for load in loads:
        load.start()

    barrier = pltpu.get_barrier_semaphore()

    @pl.loop(1, count)
    def _(step):
        pl.semaphore_signal(
            barrier,
            inc=1,
            device_id={"seq": (me + step) % count},
            device_id_type=pl.DeviceIdType.MESH,
        )

    pl.semaphore_signal(
        barrier, inc=1, device_id={"head": 1 - row}, device_id_type=pl.DeviceIdType.MESH
    )
    pl.semaphore_wait(barrier, count)

    token_copy = over(tokens_ref, arriving, token_sem.at[0], token_sem.at[1])
    token_copy.start()

    def slice_of(kind, target):
        first = (target % GROUP) * width
        if kind == 2:
            return down_ref.at[:, pl.ds(pl.multiple_of(first, width), width)]
        return gate_up_ref.at[:, pl.ds(pl.multiple_of(kind * hidden_here + first, width), width)]

    def own_slice(kind):
        return pltpu.make_async_copy(
            slice_of(kind, me), slices_ref.at[kind, 0, me], near_sem.at[kind, me]
        )

    def near(kind, source, step, target):
        return along(
            slice_of(kind, target),
            slices_ref.at[kind, 0, source],
            spread_sem.at[kind, step],
            near_sem.at[kind, source],
            target,
        )

    def cross(kind, source):
        return over(
            slices_ref.at[kind, 0, source],
            slices_ref.at[kind, 2, source],
            pass_sem.at[kind, source],
            over_sem.at[kind, source],
        )

    def twin(kind, which):
        return along(
            slices_ref.at[kind, 2 * which],
            slices_ref.at[kind, 2 * which + 1],
            twin_sem.at[kind, which, 0],
            twin_sem.at[kind, which, 1],
            partner,
        )

    place = me % GROUP
    family = me // GROUP
    families = count // GROUP

    def toward(step):
        return ((family + step // GROUP) % families) * GROUP + (place + step) % GROUP

    def away(step):
        return ((family + families - step // GROUP) % families) * GROUP + (
            place + GROUP - step % GROUP
        ) % GROUP

    def spread_steps(kind, first, end):
        @pl.loop(first, end)
        def _(step):
            near(kind, me, step, toward(step)).start()

    def spread_own(kind):
        own_slice(kind).start()
        spread_steps(kind, 1, GROUP)

    def spread_far(kind):
        spread_steps(kind, GROUP, count)

    def cross_steps(kind, first, end):
        @pl.loop(first, end)
        def _(step):
            source = away(step)
            near(kind, source, step, partner).wait_recv()
            cross(kind, source).start()

    def cross_own(kind):
        own_slice(kind).wait()
        cross(kind, me).start()
        cross_steps(kind, 1, GROUP)

    def cross_far(kind):
        cross_steps(kind, GROUP, count)
        twin(kind, 0).start()

    def cross_twin(kind):
        @pl.loop(0, count)
        def _(source):
            cross(kind, source).wait_recv()

        twin(kind, 1).start()

    def settle(kind):
        @pl.loop(1, count)
        def _(step):
            near(kind, me, step, partner).wait_send()

        @pl.loop(0, count)
        def _(source):
            cross(kind, source).wait_send()

        twin(kind, 0).wait()
        twin(kind, 1).wait()

    spread_own(0)
    spread_steps(0, GROUP + 0, GROUP + 3)
    spread_own(1)
    spread_own(2)
    def norm(source):
        wide = source[...].astype(jnp.float32)
        factor = lax.rsqrt(jnp.mean(wide * wide, axis=-1, keepdims=True) + EPSILON)
        normed[...] = (wide * factor * gain_ref[...]).astype(jnp.bfloat16)

    def turned(values, number):
        return (
            values * cos_ref[number] + pltpu.roll(values, HEAD_WIDTH // 2, 1) * sin_ref[number]
        ).astype(jnp.bfloat16)

    def project_pairs(number, half):
        for group in range(groups):
            if number == 0:
                loads[group].wait()
            pair = jnp.dot(normed[...], pair_columns[group], preferred_element_type=jnp.float32)
            key = turned(pair[:, :HEAD_WIDTH], number)
            value = pair[:, HEAD_WIDTH:].astype(jnp.bfloat16)
            staged[number, 0, group] = key
            staged[number, 1, group] = value
            key_ref[group, rows_of(half), :] = key
            value_ref[group, rows_of(half), :] = value

    def project_queries(number, half):
        for group in range(groups):
            if number == 0:
                loads[groups + group].wait()
            found = jnp.dot(normed[...], query_columns[group], preferred_element_type=jnp.float32)
            for head in range(heads):
                first = pl.multiple_of(head * 2 * height + half * height, height)
                query_ref[group, pl.ds(first, height), :] = turned(
                    found[:, head * HEAD_WIDTH : (head + 1) * HEAD_WIDTH], number
                )

    last = 2 * levels - 1

    def copy(source, index, number, half, send, target):
        return along(source, part(index, half), send, recv_sem.at[number, index], target)

    def arrived(index, number, half):
        copy(part(index, half), index, number, half, keep_sem.at[number], partner).wait_recv()

    def keep(number, half):
        return pltpu.make_async_copy(staged.at[number], part(me, half), keep_sem.at[number])

    def send_own(number, half):
        source = staged.at[number]
        pl.when(has_above)(
            lambda: copy(source, me, number, half, up_sem.at[number, 0], up).start()
        )
        pl.when(has_below)(
            lambda: copy(source, me, number, half, down_sem.at[number, 0], down).start()
        )
        copy(source, me, number, half, side_sem.at[number, 0], across).start()
        copy(source, me, number, half, core_sem.at[number, 0], partner).start()
        keep(number, half).start()

    def forward(number, half):
        for far in range(1, levels):

            @pl.when(level - far >= 0)
            def _():
                index = slot(level - far, side, core)
                arrived(index, number, half)
                block = part(index, half)
                pl.when(has_above)(
                    lambda: copy(block, index, number, half, up_sem.at[number, far], up).start()
                )
                copy(block, index, number, half, side_sem.at[number, 2 * far - 1], across).start()
                copy(block, index, number, half, core_sem.at[number, 2 * far - 1], partner).start()

            @pl.when(level + far < levels)
            def _():
                index = slot(level + far, side, core)
                arrived(index, number, half)
                block = part(index, half)
                pl.when(has_below)(
                    lambda: copy(block, index, number, half, down_sem.at[number, far], down).start()
                )
                copy(block, index, number, half, side_sem.at[number, 2 * far], across).start()
                copy(block, index, number, half, core_sem.at[number, 2 * far], partner).start()

    def pass_on(at_level, number, half, place):
        index = slot(at_level, 1 - side, core)
        arrived(index, number, half)
        copy(
            part(index, half), index, number, half, core_sem.at[number, last + place], partner
        ).start()

    def pass_all(number, half):
        pass_on(level, number, half, 0)
        for far in range(1, levels):
            pl.when(level - far >= 0)(lambda: pass_on(level - far, number, half, 2 * far - 1))
            pl.when(level + far < levels)(lambda: pass_on(level + far, number, half, 2 * far))

    def finish(number, half):
        for at_level in range(levels):
            for at_side in range(2):
                arrived(slot(at_level, at_side, 1 - core), number, half)
        keep(number, half).wait()
        source = staged.at[number]

        def sent(sem, target):
            copy(source, me, number, half, sem, target).wait_send()

        pl.when(has_above)(lambda: sent(up_sem.at[number, 0], up))
        pl.when(has_below)(lambda: sent(down_sem.at[number, 0], down))
        sent(side_sem.at[number, 0], across)
        sent(core_sem.at[number, 0], partner)
        sent(core_sem.at[number, last], partner)
        for far in range(1, levels):

            @pl.when(level - far >= 0)
            def _():
                pl.when(has_above)(lambda: sent(up_sem.at[number, far], up))
                sent(side_sem.at[number, 2 * far - 1], across)
                sent(core_sem.at[number, 2 * far - 1], partner)
                sent(core_sem.at[number, last + 2 * far - 1], partner)

            @pl.when(level + far < levels)
            def _():
                pl.when(has_below)(lambda: sent(down_sem.at[number, far], down))
                sent(side_sem.at[number, 2 * far], across)
                sent(core_sem.at[number, 2 * far], partner)
                sent(core_sem.at[number, last + 2 * far], partner)

    def attend_group(group):
        keys = jnp.concatenate(
            [pieces_ref[table_ref[back], 0, group] for back in range(window)], axis=0
        )
        values = jnp.concatenate(
            [pieces_ref[table_ref[back], 1, group] for back in range(window)], axis=0
        )
        for head in range(heads):
            query = query_ref[group, head * block : (head + 1) * block, :]
            scores = lax.dot_general(
                query, keys, (((1,), (1,)), ((), ())), preferred_element_type=jnp.float32
            )
            scores = scores * (1.0 / math.sqrt(HEAD_WIDTH)) + bias[...]
            weights = jnp.exp(scores - jnp.max(scores, axis=1, keepdims=True))
            total = jnp.sum(weights, axis=1, keepdims=True)
            mixed = jnp.dot(
                weights.astype(jnp.bfloat16), values, preferred_element_type=jnp.float32
            )
            first = (group * heads + head) * HEAD_WIDTH
            attended[:, first : first + HEAD_WIDTH] = (mixed / total).astype(jnp.bfloat16)

    pieces_out = theirs.shape[0]
    out_width = model // pieces_out

    def swap(number):
        return over(
            theirs.at[number], got.at[number], part_sem.at[0, number], part_sem.at[1, number]
        )

    def gathered(source, target_ref, number, target):
        return along(source, target_ref, rows_sem.at[0, number], rows_sem.at[1, number], target)

    half_rows = height // 2
    low = pl.ds(0, half_rows)
    high = pl.ds(half_rows, half_rows)
    climb = me + 4 - 8 * (level % 2)
    to_side = gathered(rows_ref.at[0], rows_ref.at[1], 0, across)
    to_level = gathered(rows_ref.at[0], rows_ref.at[3], 1, climb)
    side_to_level = gathered(rows_ref.at[1, low], rows_ref.at[2, low], 2, climb)
    level_to_side = gathered(rows_ref.at[3, high], rows_ref.at[2, high], 3, across)

    norm(tokens_ref)
    project_pairs(0, row)
    send_own(0, row)
    project_queries(0, row)
    token_copy.wait_recv()
    norm(arriving)
    project_pairs(1, 1 - row)
    send_own(1, 1 - row)
    project_queries(1, 1 - row)
    cross_own(0)
    cross_own(1)
    cross_own(2)
    forward(0, row)
    spread_steps(0, GROUP + 3, GROUP + 8)
    forward(1, 1 - row)
    spread_steps(1, GROUP + 0, GROUP + 6)
    pass_all(0, row)
    pass_all(1, 1 - row)
    cross_far(0)
    column = lax.broadcasted_iota(jnp.int32, bias.shape, 1)
    line = lax.broadcasted_iota(jnp.int32, bias.shape, 0)
    visible = (column >= start_ref[...]) & (column <= line + (window - 1) * block)
    bias[...] = jnp.where(visible, 0.0, -1e30)
    token_copy.wait_send()
    finish(0, row)
    finish(1, 1 - row)
    spread_steps(1, GROUP + 6, GROUP + 8)
    spread_steps(2, GROUP + 0, GROUP + 1)
    for group in range(groups):
        attend_group(group)
    loads[2 * groups].wait()
    for number in range(pieces_out):
        columns = slice(number * out_width, (number + 1) * out_width)
        theirs[number] = jnp.dot(
            attended[rows_of(1 - row), :],
            out_columns[:, columns],
            preferred_element_type=jnp.float32,
        ).astype(jnp.bfloat16)
        swap(number).start()
    for number in range(pieces_out):
        columns = slice(number * out_width, (number + 1) * out_width)
        mine[:, columns] = jnp.dot(
            attended[rows_of(row), :], out_columns[:, columns], preferred_element_type=jnp.float32
        )
    spread_steps(2, GROUP + 1, GROUP + 4)
    cross_far(1)
    cross_twin(0)
    for number in range(pieces_out):
        columns = slice(number * out_width, (number + 1) * out_width)
        swap(number).wait()
        total = tokens_ref[:, columns].astype(jnp.float32) + (
            mine[:, columns] + got[number].astype(jnp.float32)
        )
        residual_ref[:, columns] = total.astype(jnp.bfloat16)
    wide = residual_ref[...].astype(jnp.float32)
    factor = lax.rsqrt(jnp.mean(wide * wide, axis=-1, keepdims=True) + EPSILON)
    rows_ref[0] = (wide * factor * mlp_gain_ref[...]).astype(jnp.bfloat16)
    to_side.start()
    to_level.start()
    spread_steps(2, GROUP + 4, GROUP + 8)
    cross_twin(1)
    to_side.wait_recv()
    side_to_level.start()
    to_level.wait_recv()
    level_to_side.start()
    cross_far(2)
    cross_twin(2)
    side_to_level.wait()
    level_to_side.wait()
    to_side.wait_send()
    to_level.wait_send()
    for kind in range(3):
        settle(kind)


PIECES_OUT = 2


def front(tokens, gain, cosine, sine, table, starts, mlp_gain, weight, out_weight, gate_up_rows, down_rows, blocks):
    levels = blocks // 4
    height, model = tokens.shape
    heads = QUERY_HEAD_COUNT // KEY_VALUE_HEADS
    groups = weight.shape[1] // ((heads + 2) * HEAD_WIDTH)
    width = down_rows.shape[1] // GROUP
    window = table.shape[0]
    dma = pltpu.SemaphoreType.DMA
    anywhere = pl.BlockSpec(memory_space=pl.ANY)
    vmem = pl.BlockSpec(memory_space=pltpu.VMEM)
    kind = jnp.bfloat16
    return pl.pallas_call(
        functools.partial(front_kernel, levels),
        out_shape=[
            jax.ShapeDtypeStruct((4, height, model), kind),
            jax.ShapeDtypeStruct((height, model), kind),
            jax.ShapeDtypeStruct((groups, 2 * height, HEAD_WIDTH), kind),
            jax.ShapeDtypeStruct((groups, 2 * height, HEAD_WIDTH), kind),
            jax.ShapeDtypeStruct((3, 4, blocks, down_rows.shape[0], width), kind),
        ],
        in_specs=[vmem] * 4
        + [pl.BlockSpec(memory_space=pltpu.SMEM)]
        + [vmem] * 2
        + [anywhere] * 4,
        out_specs=[vmem, vmem, vmem, vmem, anywhere],
        scratch_shapes=[
            pltpu.VMEM((blocks, 2, groups, 2 * height, HEAD_WIDTH), kind),
            pltpu.VMEM((groups, heads * 2 * height, HEAD_WIDTH), kind),
            pltpu.VMEM(out_weight.shape, kind),
            pltpu.VMEM((2 * height, window * 2 * height), jnp.float32),
            pltpu.VMEM((2 * height, out_weight.shape[0]), kind),
            pltpu.VMEM((height, model), jnp.float32),
            pltpu.VMEM((PIECES_OUT, height, model // PIECES_OUT), kind),
            pltpu.VMEM((PIECES_OUT, height, model // PIECES_OUT), kind),
            pltpu.VMEM((height, model), kind),
            pltpu.VMEM((2, 2, groups, height, HEAD_WIDTH), kind),
            pltpu.VMEM((groups, model, 2 * HEAD_WIDTH), kind),
            pltpu.VMEM((groups, model, heads * HEAD_WIDTH), kind),
            pltpu.VMEM((height, model), kind),
            dma((2 * groups + 1,)),
            dma((2,)),
            dma((2,)),
            dma((2, levels)),
            dma((2, levels)),
            dma((2, 2 * levels - 1)),
            dma((2, 2 * (2 * levels - 1))),
            dma((2, blocks)),
            dma((3, blocks)),
            dma((3, blocks)),
            dma((3, blocks)),
            dma((3, blocks)),
            dma((3, 2, 2)),
            dma((2, PIECES_OUT)),
            dma((2, 4)),
        ],
        compiler_params=pltpu.CompilerParams(
            collective_id=1, has_side_effects=True, vmem_limit_bytes=60 * 1024 * 1024
        ),
        cost_estimate=pl.CostEstimate(
            flops=7 * 10**10, bytes_accessed=weight.size * 2, transcendentals=0
        ),
    )(tokens, gain, cosine, sine, table, starts, mlp_gain, weight, out_weight, gate_up_rows, down_rows)


def attention_kernel(window, table_ref, start_ref, query_ref, *refs):
    keys = refs[:window]
    values = refs[window : 2 * window]
    out_ref = refs[2 * window]
    block = keys[0].shape[-2]
    query = query_ref[0]
    heads = query.shape[0] // block
    local = jnp.concatenate([start_ref[...]] * heads, axis=0)
    row = lax.broadcasted_iota(jnp.int32, (block, 1), 0)
    row = jnp.concatenate([row] * heads, axis=0)
    key_all = jnp.concatenate([ref[0, 0, 0] for ref in keys], axis=0)
    value_all = jnp.concatenate([ref[0, 0, 0] for ref in values], axis=0)
    scores = lax.dot_general(
        query, key_all, (((1,), (1,)), ((), ())), preferred_element_type=jnp.float32
    ) * (1.0 / math.sqrt(HEAD_WIDTH))
    column = lax.broadcasted_iota(jnp.int32, scores.shape, 1)
    visible = (column >= local) & (column <= row + (window - 1) * block)
    masked = jnp.where(visible, scores, -1e30)
    top = jnp.max(masked, axis=1, keepdims=True)
    weights = jnp.exp(masked - top)
    total = jnp.sum(weights, axis=1, keepdims=True)
    mixed = jnp.dot(weights.astype(jnp.bfloat16), value_all, preferred_element_type=jnp.float32)
    out_ref[0] = (mixed / total).astype(jnp.bfloat16)


def attend(query_heads, pieces, table, local_starts, window):
    groups, rows, width = query_heads.shape
    block = local_starts.shape[0]

    def spec(kind, back):
        return pl.BlockSpec(
            (1, 1, 1, block, width),
            lambda g, table_ref: (table_ref[back], kind, g, 0, 0),
        )

    flops = 4 * groups * rows * window * block * width
    return pl.pallas_call(
        functools.partial(attention_kernel, window),
        grid_spec=pltpu.PrefetchScalarGridSpec(
            num_scalar_prefetch=1,
            grid=(groups,),
            in_specs=[
                pl.BlockSpec((block, 1), lambda g, *_: (0, 0)),
                pl.BlockSpec((1, rows, width), lambda g, *_: (g, 0, 0)),
            ]
            + [spec(0, back) for back in range(window)]
            + [spec(1, back) for back in range(window)],
            out_specs=pl.BlockSpec((1, rows, width), lambda g, *_: (g, 0, 0)),
        ),
        out_shape=jax.ShapeDtypeStruct(query_heads.shape, jnp.bfloat16),
        compiler_params=pltpu.CompilerParams(vmem_limit_bytes=48 * 1024 * 1024),
        cost_estimate=pl.CostEstimate(
            flops=flops,
            bytes_accessed=groups * (rows * 2 + window * block * 2) * width * 2,
            transcendentals=groups * rows * window * block,
        ),
    )(table, local_starts, query_heads, *([pieces] * (2 * window)))


TILE = 256


CHUNKS = 4


def mlp_kernel(
    rows_source, residual_source, slices_ref, out_ref, rows_ref, residual_ref, gates, ups, downs, hidden, held,
    first_in, second_in, sem, sum_sem,
):
    me = lax.axis_index("seq")
    across = me + 2 - 4 * ((me // 2) % 2)
    climb = me + 4 - 8 * ((me // 4) % 2)
    height = residual_ref.shape[0]
    model = residual_ref.shape[1]
    chunk_width = model // CHUNKS
    copies = []
    for kind, kept in enumerate((gates, ups, downs)):
        copies.append(
            [
                pltpu.make_async_copy(
                    slices_ref.at[kind, piece], kept.at[piece], sem.at[4 * kind + piece]
                )
                for piece in range(4)
            ]
        )
    fetch_rows = pltpu.make_async_copy(rows_source, rows_ref, sem.at[12])
    fetch_residual = pltpu.make_async_copy(residual_source, residual_ref, sem.at[13])
    fetch_rows.start()
    for piece in range(4):
        copies[0][piece].start()
        copies[1][piece].start()
    for piece in range(4):
        copies[2][piece].start()
    fetch_residual.start()
    barrier = pltpu.get_barrier_semaphore()
    for target in (across, climb):
        pl.semaphore_signal(
            barrier, inc=1, device_id={"seq": target}, device_id_type=pl.DeviceIdType.MESH
        )
    fetch_rows.wait()
    for piece in range(4):
        copies[0][piece].wait()
        gate = jnp.dot(rows_ref[...], gates[piece], preferred_element_type=jnp.float32)
        copies[1][piece].wait()
        up = jnp.dot(rows_ref[...], ups[piece], preferred_element_type=jnp.float32)
        hidden[piece] = (gate / (1.0 + jnp.exp(-gate)) * up).astype(jnp.bfloat16)
    for piece in range(4):
        copies[2][piece].wait()
    pl.semaphore_wait(barrier, 2)

    def along(source, target_ref, number, target):
        return pltpu.make_async_remote_copy(
            src_ref=source,
            dst_ref=target_ref,
            send_sem=sum_sem.at[0, number],
            recv_sem=sum_sem.at[1, number],
            device_id={"seq": target},
            device_id_type=pl.DeviceIdType.MESH,
        )

    def columns_of(chunk):
        return pl.ds(chunk * chunk_width, chunk_width)

    def block(number):
        return pl.ds(number * height, height)

    def first_hop(chunk):
        start, target = (1, across) if chunk % 2 == 0 else (2, climb)
        return along(
            held.at[pl.ds(start * height, 2 * height), columns_of(chunk)],
            first_in.at[:, columns_of(chunk)],
            chunk,
            target,
        )

    def second_hop(chunk):
        start, target = (3, climb) if chunk % 2 == 0 else (1, across)
        return along(
            held.at[block(start), columns_of(chunk)],
            second_in.at[:, columns_of(chunk)],
            CHUNKS + chunk,
            target,
        )

    def wide(ref, rows, chunk):
        return ref[rows, columns_of(chunk)].astype(jnp.float32)

    for chunk in range(CHUNKS):

        @pl.loop(0, chunk_width // TILE)
        def _(tile):
            first = pl.multiple_of(chunk * chunk_width + tile * TILE, TILE)
            total = None
            for piece in range(4):
                term = down_product(hidden[piece], downs[piece, pl.ds(first, TILE), :])
                total = term if total is None else total + term
            held[:, pl.ds(first, TILE)] = total.astype(jnp.bfloat16)

        first_hop(chunk).start()
    for chunk in range(CHUNKS):
        first_hop(chunk).wait_recv()
        passing = 3 if chunk % 2 == 0 else 1
        total = wide(held, block(passing), chunk) + wide(first_in, block(1 - chunk % 2), chunk)
        held[block(passing), columns_of(chunk)] = total.astype(jnp.bfloat16)
        second_hop(chunk).start()
    fetch_residual.wait()
    for chunk in range(CHUNKS):
        columns = columns_of(chunk)
        total = (
            residual_ref[:, columns].astype(jnp.float32)
            + wide(held, block(0), chunk)
            + wide(first_in, block(chunk % 2), chunk)
        )
        second_hop(chunk).wait_recv()
        out_ref[:, columns] = (total + second_in[:, columns].astype(jnp.float32)).astype(
            jnp.bfloat16
        )
    for chunk in range(CHUNKS):
        first_hop(chunk).wait_send()
        second_hop(chunk).wait_send()


def mlp(blocks, residual, slices):
    model = blocks.shape[2]
    width = slices.shape[3]
    height = residual.shape[0]
    rows = 4 * height
    vmem = pl.BlockSpec(memory_space=pltpu.VMEM)
    kind = jnp.bfloat16
    return pl.pallas_call(
        mlp_kernel,
        in_specs=[pl.BlockSpec(memory_space=pl.ANY)] * 3,
        out_specs=vmem,
        out_shape=jax.ShapeDtypeStruct((height, model), kind),
        scratch_shapes=[
            pltpu.VMEM((rows, model), kind),
            pltpu.VMEM((height, model), kind),
            pltpu.VMEM((4, model, width), kind),
            pltpu.VMEM((4, model, width), kind),
            pltpu.VMEM((4, model, width), kind),
            pltpu.VMEM((4, rows, width), kind),
            pltpu.VMEM((rows, model), kind),
            pltpu.VMEM((2 * height, model), kind),
            pltpu.VMEM((height, model), kind),
            pltpu.SemaphoreType.DMA((14,)),
            pltpu.SemaphoreType.DMA((2, 2 * CHUNKS)),
        ],
        compiler_params=pltpu.CompilerParams(
            collective_id=2, has_side_effects=True, vmem_limit_bytes=60 * 1024 * 1024
        ),
        cost_estimate=pl.CostEstimate(
            flops=2 * rows * model * width * 12,
            bytes_accessed=12 * model * width * 2 + 2 * rows * model * 2,
            transcendentals=rows * width * 4,
        ),
    )(blocks.reshape(rows, model), residual, slices)


def grouped_layer(
    tokens, rope_pos, inverse, table, local_starts, window, attn_gain, query_key_value_weight,
    out_weight, mlp_gain, gate_up_weight, down_weight, head_index, blocks,
):
    rows_here = tokens.shape[0]
    hidden_here = gate_up_weight.shape[2]
    angles = rope_pos.astype(jnp.float32)[:, None] * inverse[None, :]
    cosine = jnp.cos(angles)
    sine = jnp.sin(angles)

    def own_first(values):
        halves = values.reshape(2, rows_here, HEAD_WIDTH)
        return jnp.where(head_index == 0, halves, halves[::-1])

    cosine = own_first(jnp.concatenate([cosine, cosine], axis=1))
    sine = own_first(jnp.concatenate([-sine, sine], axis=1))
    gate_up_rows = gate_up_weight.reshape(gate_up_weight.shape[0], 2 * hidden_here)
    rows, residual, key_cache, value_cache, slices = front(
        tokens, attn_gain[None, :], cosine, sine, table, local_starts, mlp_gain[None, :],
        query_key_value_weight, out_weight, gate_up_rows, down_weight, blocks,
    )
    model = tokens.shape[1]
    output = mlp(rows, residual, slices.reshape(3, 4, model, slices.shape[4]))
    return (output, key_cache, value_cache)


def shards(
    tokens,
    segment_ids,
    lengths,
    deal,
    attn_gain,
    query_key_value_weight,
    out_weight,
    mlp_gain,
    gate_up_weight,
    down_weight,
):
    head_count = lax.axis_size("head")
    head_index = lax.axis_index("head")
    seq_index = lax.axis_index("seq")
    rows_here = tokens.shape[0]
    block_rows = rows_here * head_count
    heads_per_group = QUERY_HEAD_COUNT // KEY_VALUE_HEADS
    groups = query_key_value_weight.shape[1] // ((heads_per_group + 2) * HEAD_WIDTH)
    blocks = deal.shape[0]
    longest = segment_ids.shape[0] // 4
    window = min(blocks, -(-(longest - 1) // block_rows) + 1)
    hidden_here = gate_up_weight.shape[2]
    grouped = head_count == 2 and blocks % GROUP == 0 and hidden_here % (GROUP * 128) == 0
    if not grouped:
        weight_rows = jnp.concatenate(
            [gate_up_weight.reshape(gate_up_weight.shape[0], 2 * hidden_here), down_weight], axis=1
        )
        weights_all = lax.all_gather(weight_rows, "seq", axis=0, tiled=True)
    block_ids = jnp.arange(blocks, dtype=jnp.int32)
    my_block = jnp.sum(jnp.where(block_ids == seq_index, deal, 0))
    stream_pos = my_block * block_rows + jnp.arange(block_rows, dtype=jnp.int32)
    query_segments = lax.dynamic_slice_in_dim(segment_ids, my_block * block_rows, block_rows, 0)
    prompts = jnp.arange(lengths.shape[0], dtype=jnp.int32)
    starts = jnp.sum(jnp.where(prompts[None, :] < prompts[:, None], lengths[None, :], 0), axis=1)
    prompt_hits = query_segments[:, None] == jnp.arange(lengths.shape[0], dtype=jnp.int32)[None, :]
    query_starts = jnp.sum(jnp.where(prompt_hits, starts[None, :], 0), axis=1)
    rope_pos = stream_pos - query_starts
    wanted = jnp.maximum(my_block - (window - 1) + jnp.arange(window, dtype=jnp.int32), 0)
    table = jnp.sum(
        jnp.where(wanted[:, None] == deal[None, :], block_ids[None, :], 0), axis=1
    ).astype(jnp.int32)
    local_starts = (query_starts - (my_block - (window - 1)) * block_rows)[:, None]
    inverse = frequencies(HEAD_WIDTH)
    if grouped:
        return grouped_layer(
            tokens, rope_pos, inverse, table, local_starts, window, attn_gain, query_key_value_weight,
            out_weight, mlp_gain, gate_up_weight, down_weight, head_index, blocks,
        )
    full_rows = jnp.zeros((block_rows, tokens.shape[1]), tokens.dtype)
    full_rows = lax.dynamic_update_slice_in_dim(full_rows, tokens, head_index * rows_here, 0)
    for step in range(1, head_count):
        source = (head_index - step) % head_count
        full_rows = lax.dynamic_update_slice_in_dim(
            full_rows, shift(tokens, step, head_count), source * rows_here, 0
        )
    projected_rows = jnp.dot(
        normalize(full_rows, attn_gain), query_key_value_weight, preferred_element_type=jnp.float32
    )
    projected_rows = projected_rows.reshape(block_rows, groups, heads_per_group + 2, HEAD_WIDTH)
    queries = rotate(projected_rows[:, :, :heads_per_group], rope_pos, inverse).astype(jnp.bfloat16)
    key_matrix = rotate(
        projected_rows[:, :, heads_per_group : heads_per_group + 1], rope_pos, inverse
    )[:, :, 0].astype(jnp.bfloat16)
    value_matrix = projected_rows[:, :, heads_per_group + 1].astype(jnp.bfloat16)
    key_cache = jnp.transpose(key_matrix, (1, 0, 2))
    value_cache = jnp.transpose(value_matrix, (1, 0, 2))
    query_heads = jnp.transpose(queries, (1, 2, 0, 3)).reshape(
        groups, heads_per_group * block_rows, HEAD_WIDTH
    )
    key_value = jnp.stack([key_cache, value_cache])
    pieces = gather_blocks(key_value, blocks)
    attended = attend(query_heads, pieces, table, local_starts, window)
    attended = jnp.transpose(
        attended.reshape(groups, heads_per_group, block_rows, HEAD_WIDTH), (2, 0, 1, 3)
    ).reshape(block_rows, groups * heads_per_group * HEAD_WIDTH)
    part = jnp.dot(attended, out_weight, preferred_element_type=jnp.float32).astype(jnp.bfloat16)
    total_proj = part.astype(jnp.float32)
    for step in range(1, head_count):
        total_proj = total_proj + shift(part, step, head_count).astype(jnp.float32)
    full_residual = (full_rows.astype(jnp.float32) + total_proj).astype(jnp.bfloat16)
    mlp_in = lax.optimization_barrier(normalize(full_residual, mlp_gain))
    residual = lax.dynamic_slice_in_dim(full_residual, head_index * rows_here, rows_here, 0)
    gate = jnp.dot(mlp_in, weights_all[:, :hidden_here], preferred_element_type=jnp.float32)
    up = jnp.dot(
        mlp_in, weights_all[:, hidden_here : 2 * hidden_here], preferred_element_type=jnp.float32
    )
    hidden = (jax.nn.silu(gate) * up).astype(jnp.bfloat16)
    chunks = []
    pieces_down = 3
    width = weights_all.shape[0] // pieces_down
    for number in range(pieces_down):
        columns = slice(number * width, (number + 1) * width)
        terms = down_product(hidden, weights_all[columns, 2 * hidden_here :]).astype(jnp.bfloat16)
        total = residual[:, columns].astype(jnp.float32) + lax.dynamic_slice_in_dim(
            terms, head_index * rows_here, rows_here, 0
        ).astype(jnp.float32)
        for step in range(1, head_count):
            target = (head_index + step) % head_count
            piece = lax.dynamic_slice_in_dim(terms, target * rows_here, rows_here, 0)
            total = total + shift(piece, step, head_count).astype(jnp.float32)
        chunks.append(total.astype(jnp.bfloat16))
    output = jnp.concatenate(chunks, axis=1)
    return (output, key_cache, value_cache)


def solution(mesh):
    placed = (
        P(("seq", "head"), None),
        P(),
        P(),
        P(),
        P(),
        P(None, "head"),
        P("head", None),
        P(),
        P("seq", None, "head"),
        P("seq", "head"),
    )
    return jax.shard_map(
        shards,
        mesh=mesh,
        in_specs=placed,
        out_specs=(P(("seq", "head"), None), P("head", "seq", None), P("head", "seq", None)),
        check_vma=False,
    )
```

```python
import functools
import math

import jax
import jax.numpy as jnp
from jax import lax
from jax.experimental import pallas as pl
from jax.experimental.pallas import tpu as pltpu
from jax.sharding import PartitionSpec as P

QUERY_HEAD_COUNT = 24
KEY_VALUE_HEADS = 8
HEAD_WIDTH = 128


EPSILON = 1e-05
CORE = 1
SIDE = 2
LEVEL = 4
GROUP = 8
ROPE_BASE = 500000.0


def frequencies(head_size):
    exponent = jnp.arange(0, head_size, 2, dtype=jnp.float32) / head_size
    inverse = 1.0 / ROPE_BASE**exponent
    wavelength = 2.0 * math.pi / inverse
    smooth = (8192.0 / wavelength - 1.0) / 3.0
    blended = (1.0 - smooth) * inverse / 32.0 + smooth * inverse
    return jnp.where(
        wavelength > 8192.0, inverse / 32.0, jnp.where(wavelength < 2048.0, inverse, blended)
    )


def rotate(row_values, position, inverse):
    angles = position.astype(jnp.float32)[:, None] * inverse[None, :]
    cosine = jnp.cos(angles)[:, None, None, :]
    sine_term = jnp.sin(angles)[:, None, None, :]
    half_size = row_values.shape[-1] // 2
    first_half = row_values[..., :half_size]
    second_half = row_values[..., half_size:]
    return jnp.concatenate(
        [
            first_half * cosine - second_half * sine_term,
            second_half * cosine + first_half * sine_term,
        ],
        axis=-1,
    )


def normalize(row_values, gain_vector):
    values_wide = row_values.astype(jnp.float32)
    factor = lax.rsqrt(jnp.mean(values_wide * values_wide, axis=-1, keepdims=True) + EPSILON)
    return (values_wide * factor * gain_vector).astype(jnp.bfloat16)


def down_product(hidden, down_rows):
    return lax.dot_general(
        hidden, down_rows, (((1,), (1,)), ((), ())), preferred_element_type=jnp.float32
    )


def shift(values, step, count):
    return lax.ppermute(values, "head", [(i, (i + step) % count) for i in range(count)])


def gather_kernel(levels, own_ref, out_ref, copy_sem, up_sem, down_sem, side_sem, core_sem, recv_sem):
    me = lax.axis_index("seq")
    core = me % 2
    side = (me // 2) % 2
    level = me // 4
    has_above = level < levels - 1
    has_below = level > 0

    def slot(at_level, at_side, at_core):
        return at_level * 4 + at_side * 2 + at_core

    up = me + 4
    down = me - 4
    across = me + 2 - 4 * side
    partner = me + 1 - 2 * core

    def copy(source, index, send_sem, target):
        return pltpu.make_async_remote_copy(
            src_ref=source,
            dst_ref=out_ref.at[index],
            send_sem=send_sem,
            recv_sem=recv_sem.at[index],
            device_id={"seq": target},
            device_id_type=pl.DeviceIdType.MESH,
        )

    def arrived(index):
        copy(out_ref.at[index], index, copy_sem, partner).wait_recv()

    def greet(target):
        pl.semaphore_signal(
            barrier, inc=1, device_id={"seq": target}, device_id_type=pl.DeviceIdType.MESH
        )

    barrier = pltpu.get_barrier_semaphore()
    greet(partner)
    greet(across)
    pl.when(has_above)(lambda: greet(up))
    pl.when(has_below)(lambda: greet(down))
    peers = 2 + jnp.where(has_above, 1, 0) + jnp.where(has_below, 1, 0)
    pl.semaphore_wait(barrier, peers)

    pl.when(has_above)(lambda: copy(own_ref, me, up_sem.at[0], up).start())
    pl.when(has_below)(lambda: copy(own_ref, me, down_sem.at[0], down).start())
    copy(own_ref, me, side_sem.at[0], across).start()
    copy(own_ref, me, core_sem.at[0], partner).start()
    keep = pltpu.make_async_copy(own_ref, out_ref.at[me], copy_sem)
    keep.start()

    for far in range(1, levels):

        @pl.when(level - far >= 0)
        def _():
            index = slot(level - far, side, core)
            arrived(index)
            block = out_ref.at[index]
            pl.when(has_above)(lambda: copy(block, index, up_sem.at[far], up).start())
            copy(block, index, side_sem.at[2 * far - 1], across).start()
            copy(block, index, core_sem.at[2 * far - 1], partner).start()

        @pl.when(level + far < levels)
        def _():
            index = slot(level + far, side, core)
            arrived(index)
            block = out_ref.at[index]
            pl.when(has_below)(lambda: copy(block, index, down_sem.at[far], down).start())
            copy(block, index, side_sem.at[2 * far], across).start()
            copy(block, index, core_sem.at[2 * far], partner).start()

    offset = 2 * levels - 1

    def pass_on(at_level, number):
        index = slot(at_level, 1 - side, core)
        arrived(index)
        copy(out_ref.at[index], index, core_sem.at[offset + number], partner).start()

    pass_on(level, 0)
    for far in range(1, levels):
        pl.when(level - far >= 0)(lambda: pass_on(level - far, 2 * far - 1))
        pl.when(level + far < levels)(lambda: pass_on(level + far, 2 * far))

    for at_level in range(levels):
        for at_side in range(2):
            arrived(slot(at_level, at_side, 1 - core))

    keep.wait()

    def sent(sem, target):
        copy(own_ref, me, sem, target).wait_send()

    pl.when(has_above)(lambda: sent(up_sem.at[0], up))
    pl.when(has_below)(lambda: sent(down_sem.at[0], down))
    sent(side_sem.at[0], across)
    sent(core_sem.at[0], partner)
    sent(core_sem.at[offset], partner)
    for far in range(1, levels):

        @pl.when(level - far >= 0)
        def _():
            pl.when(has_above)(lambda: sent(up_sem.at[far], up))
            sent(side_sem.at[2 * far - 1], across)
            sent(core_sem.at[2 * far - 1], partner)
            sent(core_sem.at[offset + 2 * far - 1], partner)

        @pl.when(level + far < levels)
        def _():
            pl.when(has_below)(lambda: sent(down_sem.at[far], down))
            sent(side_sem.at[2 * far], across)
            sent(core_sem.at[2 * far], partner)
            sent(core_sem.at[offset + 2 * far], partner)


def gather_blocks(own, count):
    levels = count // 4
    dma = pltpu.SemaphoreType.DMA
    return pl.pallas_call(
        functools.partial(gather_kernel, levels),
        out_shape=jax.ShapeDtypeStruct((count,) + own.shape, own.dtype),
        in_specs=[pl.BlockSpec(memory_space=pl.ANY)],
        out_specs=pl.BlockSpec(memory_space=pl.ANY),
        scratch_shapes=[
            dma,
            dma((levels,)),
            dma((levels,)),
            dma((2 * levels - 1,)),
            dma((2 * (2 * levels - 1),)),
            dma((count,)),
        ],
        compiler_params=pltpu.CompilerParams(collective_id=0, has_side_effects=True),
        cost_estimate=pl.CostEstimate(flops=7 * 10**10, bytes_accessed=count * own.size * 2, transcendentals=0),
    )(own)


def front_kernel(
    levels,
    tokens_ref,
    gain_ref,
    cos_ref,
    sin_ref,
    table_ref,
    start_ref,
    mlp_gain_ref,
    weight_ref,
    out_weight_ref,
    gate_up_ref,
    down_ref,
    rows_ref,
    residual_ref,
    key_ref,
    value_ref,
    slices_ref,
    pieces_ref,
    query_ref,
    out_columns,
    bias,
    attended,
    mine,
    theirs,
    got,
    arriving,
    staged,
    pair_columns,
    query_columns,
    normed,
    load_sem,
    keep_sem,
    token_sem,
    up_sem,
    down_sem,
    side_sem,
    core_sem,
    recv_sem,
    spread_sem,
    near_sem,
    pass_sem,
    over_sem,
    twin_sem,
    part_sem,
    rows_sem,
):
    count = 4 * levels
    me = lax.axis_index("seq")
    row = lax.axis_index("head")
    core = me % 2
    side = (me // 2) % 2
    level = me // 4
    has_above = level < levels - 1
    has_below = level > 0
    up = me + 4
    down = me - 4
    across = me + 2 - 4 * side
    partner = me + 1 - 2 * core
    height = tokens_ref.shape[0]
    groups = pair_columns.shape[0]
    heads = query_columns.shape[2] // HEAD_WIDTH
    span = (heads + 2) * HEAD_WIDTH
    width = slices_ref.shape[4]
    hidden_here = down_ref.shape[1]
    model = tokens_ref.shape[1]
    window = table_ref.shape[0]
    block = 2 * height

    def slot(at_level, at_side, at_core):
        return at_level * 4 + at_side * 2 + at_core

    def rows_of(half):
        return pl.ds(pl.multiple_of(half * height, height), height)

    def part(index, half):
        return pieces_ref.at[index, :, :, rows_of(half), :]

    def along(source, target_ref, send, recv, target):
        return pltpu.make_async_remote_copy(
            src_ref=source,
            dst_ref=target_ref,
            send_sem=send,
            recv_sem=recv,
            device_id={"seq": target},
            device_id_type=pl.DeviceIdType.MESH,
        )

    def over(source, target_ref, send, recv):
        return pltpu.make_async_remote_copy(
            src_ref=source,
            dst_ref=target_ref,
            send_sem=send,
            recv_sem=recv,
            device_id={"head": 1 - row},
            device_id_type=pl.DeviceIdType.MESH,
        )

    loads = []
    for group in range(groups):
        loads.append(
            pltpu.make_async_copy(
                weight_ref.at[:, pl.ds(group * span + heads * HEAD_WIDTH, 2 * HEAD_WIDTH)],
                pair_columns.at[group],
                load_sem.at[group],
            )
        )
    for group in range(groups):
        loads.append(
            pltpu.make_async_copy(
                weight_ref.at[:, pl.ds(group * span, heads * HEAD_WIDTH)],
                query_columns.at[group],
                load_sem.at[groups + group],
            )
        )
    loads.append(
        pltpu.make_async_copy(out_weight_ref, out_columns, load_sem.at[2 * groups])
    )
    for load in loads:
        load.start()

    barrier = pltpu.get_barrier_semaphore()

    @pl.loop(1, count)
    def _(step):
        pl.semaphore_signal(
            barrier,
            inc=1,
            device_id={"seq": (me + step) % count},
            device_id_type=pl.DeviceIdType.MESH,
        )

    pl.semaphore_signal(
        barrier, inc=1, device_id={"head": 1 - row}, device_id_type=pl.DeviceIdType.MESH
    )
    pl.semaphore_wait(barrier, count)

    token_copy = over(tokens_ref, arriving, token_sem.at[0], token_sem.at[1])
    token_copy.start()

    def slice_of(kind, target):
        first = (target % GROUP) * width
        if kind == 2:
            return down_ref.at[:, pl.ds(pl.multiple_of(first, width), width)]
        return gate_up_ref.at[:, pl.ds(pl.multiple_of(kind * hidden_here + first, width), width)]

    def own_slice(kind):
        return pltpu.make_async_copy(
            slice_of(kind, me), slices_ref.at[kind, 0, me], near_sem.at[kind, me]
        )

    def near(kind, source, step, target):
        return along(
            slice_of(kind, target),
            slices_ref.at[kind, 0, source],
            spread_sem.at[kind, step],
            near_sem.at[kind, source],
            target,
        )

    def cross(kind, source):
        return over(
            slices_ref.at[kind, 0, source],
            slices_ref.at[kind, 2, source],
            pass_sem.at[kind, source],
            over_sem.at[kind, source],
        )

    def twin(kind, which):
        return along(
            slices_ref.at[kind, 2 * which],
            slices_ref.at[kind, 2 * which + 1],
            twin_sem.at[kind, which, 0],
            twin_sem.at[kind, which, 1],
            partner,
        )

    place = me % GROUP
    family = me // GROUP
    families = count // GROUP

    def toward(step):
        return ((family + step // GROUP) % families) * GROUP + (place + step) % GROUP

    def away(step):
        return ((family + families - step // GROUP) % families) * GROUP + (
            place + GROUP - step % GROUP
        ) % GROUP

    def spread_steps(kind, first, end):
        @pl.loop(first, end)
        def _(step):
            near(kind, me, step, toward(step)).start()

    def spread_own(kind):
        own_slice(kind).start()
        spread_steps(kind, 1, GROUP)

    def spread_far(kind):
        spread_steps(kind, GROUP, count)

    def cross_steps(kind, first, end):
        @pl.loop(first, end)
        def _(step):
            source = away(step)
            near(kind, source, step, partner).wait_recv()
            cross(kind, source).start()

    def cross_own(kind):
        own_slice(kind).wait()
        cross(kind, me).start()
        cross_steps(kind, 1, GROUP)

    def cross_far(kind):
        cross_steps(kind, GROUP, count)
        twin(kind, 0).start()

    def cross_twin(kind):
        @pl.loop(0, count)
        def _(source):
            cross(kind, source).wait_recv()

        twin(kind, 1).start()

    def settle(kind):
        @pl.loop(1, count)
        def _(step):
            near(kind, me, step, partner).wait_send()

        @pl.loop(0, count)
        def _(source):
            cross(kind, source).wait_send()

        twin(kind, 0).wait()
        twin(kind, 1).wait()

    spread_own(0)
    spread_steps(0, GROUP + 0, GROUP + 3)
    spread_own(1)
    spread_own(2)
    def norm(source):
        wide = source[...].astype(jnp.float32)
        factor = lax.rsqrt(jnp.mean(wide * wide, axis=-1, keepdims=True) + EPSILON)
        normed[...] = (wide * factor * gain_ref[...]).astype(jnp.bfloat16)

    def turned(values, half):
        return (
            values * cos_ref[half] + pltpu.roll(values, HEAD_WIDTH // 2, 1) * sin_ref[half]
        ).astype(jnp.bfloat16)

    def project_pairs(number, half):
        for group in range(groups):
            if number == 0:
                loads[group].wait()
            pair = jnp.dot(normed[...], pair_columns[group], preferred_element_type=jnp.float32)
            key = turned(pair[:, :HEAD_WIDTH], half)
            value = pair[:, HEAD_WIDTH:].astype(jnp.bfloat16)
            staged[number, 0, group] = key
            staged[number, 1, group] = value
            key_ref[group, rows_of(half), :] = key
            value_ref[group, rows_of(half), :] = value

    def project_queries(number, half):
        for group in range(groups):
            if number == 0:
                loads[groups + group].wait()
            found = jnp.dot(normed[...], query_columns[group], preferred_element_type=jnp.float32)
            for head in range(heads):
                first = pl.multiple_of(head * 2 * height + half * height, height)
                query_ref[group, pl.ds(first, height), :] = turned(
                    found[:, head * HEAD_WIDTH : (head + 1) * HEAD_WIDTH], half
                )

    last = 2 * levels - 1

    def copy(source, index, number, half, send, target):
        return along(source, part(index, half), send, recv_sem.at[number, index], target)

    def arrived(index, number, half):
        copy(part(index, half), index, number, half, keep_sem.at[number], partner).wait_recv()

    def keep(number, half):
        return pltpu.make_async_copy(staged.at[number], part(me, half), keep_sem.at[number])

    def send_own(number, half):
        source = staged.at[number]
        pl.when(has_above)(
            lambda: copy(source, me, number, half, up_sem.at[number, 0], up).start()
        )
        pl.when(has_below)(
            lambda: copy(source, me, number, half, down_sem.at[number, 0], down).start()
        )
        copy(source, me, number, half, side_sem.at[number, 0], across).start()
        copy(source, me, number, half, core_sem.at[number, 0], partner).start()
        keep(number, half).start()

    def forward(number, half):
        for far in range(1, levels):

            @pl.when(level - far >= 0)
            def _():
                index = slot(level - far, side, core)
                arrived(index, number, half)
                block = part(index, half)
                pl.when(has_above)(
                    lambda: copy(block, index, number, half, up_sem.at[number, far], up).start()
                )
                copy(block, index, number, half, side_sem.at[number, 2 * far - 1], across).start()
                copy(block, index, number, half, core_sem.at[number, 2 * far - 1], partner).start()

            @pl.when(level + far < levels)
            def _():
                index = slot(level + far, side, core)
                arrived(index, number, half)
                block = part(index, half)
                pl.when(has_below)(
                    lambda: copy(block, index, number, half, down_sem.at[number, far], down).start()
                )
                copy(block, index, number, half, side_sem.at[number, 2 * far], across).start()
                copy(block, index, number, half, core_sem.at[number, 2 * far], partner).start()

    def pass_on(at_level, number, half, place):
        index = slot(at_level, 1 - side, core)
        arrived(index, number, half)
        copy(
            part(index, half), index, number, half, core_sem.at[number, last + place], partner
        ).start()

    def pass_all(number, half):
        pass_on(level, number, half, 0)
        for far in range(1, levels):
            pl.when(level - far >= 0)(lambda: pass_on(level - far, number, half, 2 * far - 1))
            pl.when(level + far < levels)(lambda: pass_on(level + far, number, half, 2 * far))

    def finish(number, half):
        for at_level in range(levels):
            for at_side in range(2):
                arrived(slot(at_level, at_side, 1 - core), number, half)
        keep(number, half).wait()
        source = staged.at[number]

        def sent(sem, target):
            copy(source, me, number, half, sem, target).wait_send()

        pl.when(has_above)(lambda: sent(up_sem.at[number, 0], up))
        pl.when(has_below)(lambda: sent(down_sem.at[number, 0], down))
        sent(side_sem.at[number, 0], across)
        sent(core_sem.at[number, 0], partner)
        sent(core_sem.at[number, last], partner)
        for far in range(1, levels):

            @pl.when(level - far >= 0)
            def _():
                pl.when(has_above)(lambda: sent(up_sem.at[number, far], up))
                sent(side_sem.at[number, 2 * far - 1], across)
                sent(core_sem.at[number, 2 * far - 1], partner)
                sent(core_sem.at[number, last + 2 * far - 1], partner)

            @pl.when(level + far < levels)
            def _():
                pl.when(has_below)(lambda: sent(down_sem.at[number, far], down))
                sent(side_sem.at[number, 2 * far], across)
                sent(core_sem.at[number, 2 * far], partner)
                sent(core_sem.at[number, last + 2 * far], partner)

    def attend_group(group):
        keys = jnp.concatenate(
            [pieces_ref[table_ref[back], 0, group] for back in range(window)], axis=0
        )
        values = jnp.concatenate(
            [pieces_ref[table_ref[back], 1, group] for back in range(window)], axis=0
        )
        for head in range(heads):
            query = query_ref[group, head * block : (head + 1) * block, :]
            scores = lax.dot_general(
                query, keys, (((1,), (1,)), ((), ())), preferred_element_type=jnp.float32
            )
            scores = scores * (1.0 / math.sqrt(HEAD_WIDTH)) + bias[...]
            weights = jnp.exp(scores - jnp.max(scores, axis=1, keepdims=True))
            total = jnp.sum(weights, axis=1, keepdims=True)
            mixed = jnp.dot(
                weights.astype(jnp.bfloat16), values, preferred_element_type=jnp.float32
            )
            first = (group * heads + head) * HEAD_WIDTH
            attended[:, first : first + HEAD_WIDTH] = (mixed / total).astype(jnp.bfloat16)

    pieces_out = theirs.shape[0]
    out_width = model // pieces_out

    def swap(number):
        return over(
            theirs.at[number], got.at[number], part_sem.at[0, number], part_sem.at[1, number]
        )

    def gathered(source, target_ref, number, target):
        return along(source, target_ref, rows_sem.at[0, number], rows_sem.at[1, number], target)

    half_rows = height // 2
    low = pl.ds(0, half_rows)
    high = pl.ds(half_rows, half_rows)
    climb = me + 4 - 8 * (level % 2)
    to_side = gathered(rows_ref.at[0], rows_ref.at[1], 0, across)
    to_level = gathered(rows_ref.at[0], rows_ref.at[3], 1, climb)
    side_to_level = gathered(rows_ref.at[1, low], rows_ref.at[2, low], 2, climb)
    level_to_side = gathered(rows_ref.at[3, high], rows_ref.at[2, high], 3, across)

    norm(tokens_ref)
    project_pairs(0, row)
    send_own(0, row)
    project_queries(0, row)
    token_copy.wait_recv()
    norm(arriving)
    project_pairs(1, 1 - row)
    send_own(1, 1 - row)
    project_queries(1, 1 - row)
    cross_own(0)
    cross_own(1)
    cross_own(2)
    forward(0, row)
    spread_steps(0, GROUP + 3, GROUP + 8)
    forward(1, 1 - row)
    spread_steps(1, GROUP + 0, GROUP + 6)
    pass_all(0, row)
    pass_all(1, 1 - row)
    cross_far(0)
    column = lax.broadcasted_iota(jnp.int32, bias.shape, 1)
    line = lax.broadcasted_iota(jnp.int32, bias.shape, 0)
    visible = (column >= start_ref[...]) & (column <= line + (window - 1) * block)
    bias[...] = jnp.where(visible, 0.0, -1e30)
    token_copy.wait_send()
    finish(0, row)
    finish(1, 1 - row)
    spread_steps(1, GROUP + 6, GROUP + 8)
    spread_steps(2, GROUP + 0, GROUP + 1)
    for group in range(groups):
        attend_group(group)
    loads[2 * groups].wait()
    for number in range(pieces_out):
        columns = slice(number * out_width, (number + 1) * out_width)
        theirs[number] = jnp.dot(
            attended[rows_of(1 - row), :],
            out_columns[:, columns],
            preferred_element_type=jnp.float32,
        ).astype(jnp.bfloat16)
        swap(number).start()
    for number in range(pieces_out):
        columns = slice(number * out_width, (number + 1) * out_width)
        mine[:, columns] = jnp.dot(
            attended[rows_of(row), :], out_columns[:, columns], preferred_element_type=jnp.float32
        )
    spread_steps(2, GROUP + 1, GROUP + 4)
    cross_far(1)
    cross_twin(0)
    for number in range(pieces_out):
        columns = slice(number * out_width, (number + 1) * out_width)
        swap(number).wait()
        total = tokens_ref[:, columns].astype(jnp.float32) + (
            mine[:, columns] + got[number].astype(jnp.float32)
        )
        residual_ref[:, columns] = total.astype(jnp.bfloat16)
    wide = residual_ref[...].astype(jnp.float32)
    factor = lax.rsqrt(jnp.mean(wide * wide, axis=-1, keepdims=True) + EPSILON)
    rows_ref[0] = (wide * factor * mlp_gain_ref[...]).astype(jnp.bfloat16)
    to_side.start()
    to_level.start()
    spread_steps(2, GROUP + 4, GROUP + 8)
    cross_twin(1)
    to_side.wait_recv()
    side_to_level.start()
    to_level.wait_recv()
    level_to_side.start()
    cross_far(2)
    cross_twin(2)
    side_to_level.wait()
    level_to_side.wait()
    to_side.wait_send()
    to_level.wait_send()
    for kind in range(3):
        settle(kind)


PIECES_OUT = 2


def front(tokens, gain, cosine, sine, table, starts, mlp_gain, weight, out_weight, gate_up_rows, down_rows, blocks):
    levels = blocks // 4
    height, model = tokens.shape
    heads = QUERY_HEAD_COUNT // KEY_VALUE_HEADS
    groups = weight.shape[1] // ((heads + 2) * HEAD_WIDTH)
    width = down_rows.shape[1] // GROUP
    window = table.shape[0]
    dma = pltpu.SemaphoreType.DMA
    anywhere = pl.BlockSpec(memory_space=pl.ANY)
    vmem = pl.BlockSpec(memory_space=pltpu.VMEM)
    kind = jnp.bfloat16
    return pl.pallas_call(
        functools.partial(front_kernel, levels),
        out_shape=[
            jax.ShapeDtypeStruct((4, height, model), kind),
            jax.ShapeDtypeStruct((height, model), kind),
            jax.ShapeDtypeStruct((groups, 2 * height, HEAD_WIDTH), kind),
            jax.ShapeDtypeStruct((groups, 2 * height, HEAD_WIDTH), kind),
            jax.ShapeDtypeStruct((3, 4, blocks, down_rows.shape[0], width), kind),
        ],
        in_specs=[vmem] * 4
        + [pl.BlockSpec(memory_space=pltpu.SMEM)]
        + [vmem] * 2
        + [anywhere] * 4,
        out_specs=[vmem, vmem, vmem, vmem, anywhere],
        scratch_shapes=[
            pltpu.VMEM((blocks, 2, groups, 2 * height, HEAD_WIDTH), kind),
            pltpu.VMEM((groups, heads * 2 * height, HEAD_WIDTH), kind),
            pltpu.VMEM(out_weight.shape, kind),
            pltpu.VMEM((2 * height, window * 2 * height), jnp.float32),
            pltpu.VMEM((2 * height, out_weight.shape[0]), kind),
            pltpu.VMEM((height, model), jnp.float32),
            pltpu.VMEM((PIECES_OUT, height, model // PIECES_OUT), kind),
            pltpu.VMEM((PIECES_OUT, height, model // PIECES_OUT), kind),
            pltpu.VMEM((height, model), kind),
            pltpu.VMEM((2, 2, groups, height, HEAD_WIDTH), kind),
            pltpu.VMEM((groups, model, 2 * HEAD_WIDTH), kind),
            pltpu.VMEM((groups, model, heads * HEAD_WIDTH), kind),
            pltpu.VMEM((height, model), kind),
            dma((2 * groups + 1,)),
            dma((2,)),
            dma((2,)),
            dma((2, levels)),
            dma((2, levels)),
            dma((2, 2 * levels - 1)),
            dma((2, 2 * (2 * levels - 1))),
            dma((2, blocks)),
            dma((3, blocks)),
            dma((3, blocks)),
            dma((3, blocks)),
            dma((3, blocks)),
            dma((3, 2, 2)),
            dma((2, PIECES_OUT)),
            dma((2, 4)),
        ],
        compiler_params=pltpu.CompilerParams(
            collective_id=1, has_side_effects=True, vmem_limit_bytes=60 * 1024 * 1024
        ),
        cost_estimate=pl.CostEstimate(
            flops=7 * 10**10, bytes_accessed=weight.size * 2, transcendentals=0
        ),
    )(tokens, gain, cosine, sine, table, starts, mlp_gain, weight, out_weight, gate_up_rows, down_rows)


def attention_kernel(window, table_ref, start_ref, query_ref, *refs):
    keys = refs[:window]
    values = refs[window : 2 * window]
    out_ref = refs[2 * window]
    block = keys[0].shape[-2]
    query = query_ref[0]
    heads = query.shape[0] // block
    local = jnp.concatenate([start_ref[...]] * heads, axis=0)
    row = lax.broadcasted_iota(jnp.int32, (block, 1), 0)
    row = jnp.concatenate([row] * heads, axis=0)
    key_all = jnp.concatenate([ref[0, 0, 0] for ref in keys], axis=0)
    value_all = jnp.concatenate([ref[0, 0, 0] for ref in values], axis=0)
    scores = lax.dot_general(
        query, key_all, (((1,), (1,)), ((), ())), preferred_element_type=jnp.float32
    ) * (1.0 / math.sqrt(HEAD_WIDTH))
    column = lax.broadcasted_iota(jnp.int32, scores.shape, 1)
    visible = (column >= local) & (column <= row + (window - 1) * block)
    masked = jnp.where(visible, scores, -1e30)
    top = jnp.max(masked, axis=1, keepdims=True)
    weights = jnp.exp(masked - top)
    total = jnp.sum(weights, axis=1, keepdims=True)
    mixed = jnp.dot(weights.astype(jnp.bfloat16), value_all, preferred_element_type=jnp.float32)
    out_ref[0] = (mixed / total).astype(jnp.bfloat16)


def attend(query_heads, pieces, table, local_starts, window):
    groups, rows, width = query_heads.shape
    block = local_starts.shape[0]

    def spec(kind, back):
        return pl.BlockSpec(
            (1, 1, 1, block, width),
            lambda g, table_ref: (table_ref[back], kind, g, 0, 0),
        )

    flops = 4 * groups * rows * window * block * width
    return pl.pallas_call(
        functools.partial(attention_kernel, window),
        grid_spec=pltpu.PrefetchScalarGridSpec(
            num_scalar_prefetch=1,
            grid=(groups,),
            in_specs=[
                pl.BlockSpec((block, 1), lambda g, *_: (0, 0)),
                pl.BlockSpec((1, rows, width), lambda g, *_: (g, 0, 0)),
            ]
            + [spec(0, back) for back in range(window)]
            + [spec(1, back) for back in range(window)],
            out_specs=pl.BlockSpec((1, rows, width), lambda g, *_: (g, 0, 0)),
        ),
        out_shape=jax.ShapeDtypeStruct(query_heads.shape, jnp.bfloat16),
        compiler_params=pltpu.CompilerParams(vmem_limit_bytes=48 * 1024 * 1024),
        cost_estimate=pl.CostEstimate(
            flops=flops,
            bytes_accessed=groups * (rows * 2 + window * block * 2) * width * 2,
            transcendentals=groups * rows * window * block,
        ),
    )(table, local_starts, query_heads, *([pieces] * (2 * window)))


TILE = 256


CHUNKS = 12


def mlp_kernel(
    rows_source, residual_source, slices_ref, out_ref, rows_ref, residual_ref, gates, ups, downs, hidden, held,
    first_in, second_in, sem, sum_sem,
):
    me = lax.axis_index("seq")
    across = me + 2 - 4 * ((me // 2) % 2)
    climb = me + 4 - 8 * ((me // 4) % 2)
    height = residual_ref.shape[0]
    model = residual_ref.shape[1]
    chunk_width = model // CHUNKS
    copies = []
    for kind, kept in enumerate((gates, ups, downs)):
        copies.append(
            [
                pltpu.make_async_copy(
                    slices_ref.at[kind, piece], kept.at[piece], sem.at[4 * kind + piece]
                )
                for piece in range(4)
            ]
        )
    fetch_rows = pltpu.make_async_copy(rows_source, rows_ref, sem.at[12])
    fetch_residual = pltpu.make_async_copy(residual_source, residual_ref, sem.at[13])
    fetch_rows.start()
    for piece in range(4):
        copies[0][piece].start()
        copies[1][piece].start()
    for piece in range(4):
        copies[2][piece].start()
    fetch_residual.start()
    barrier = pltpu.get_barrier_semaphore()
    for target in (across, climb):
        pl.semaphore_signal(
            barrier, inc=1, device_id={"seq": target}, device_id_type=pl.DeviceIdType.MESH
        )
    fetch_rows.wait()
    for piece in range(4):
        copies[0][piece].wait()
        gate = jnp.dot(rows_ref[...], gates[piece], preferred_element_type=jnp.float32)
        copies[1][piece].wait()
        up = jnp.dot(rows_ref[...], ups[piece], preferred_element_type=jnp.float32)
        hidden[piece] = (gate / (1.0 + jnp.exp(-gate)) * up).astype(jnp.bfloat16)
    for piece in range(4):
        copies[2][piece].wait()
    pl.semaphore_wait(barrier, 2)

    def along(source, target_ref, number, target):
        return pltpu.make_async_remote_copy(
            src_ref=source,
            dst_ref=target_ref,
            send_sem=sum_sem.at[0, number],
            recv_sem=sum_sem.at[1, number],
            device_id={"seq": target},
            device_id_type=pl.DeviceIdType.MESH,
        )

    def columns_of(chunk):
        return pl.ds(chunk * chunk_width, chunk_width)

    def block(number):
        return pl.ds(number * height, height)

    def first_hop(chunk):
        start, target = (1, across) if chunk % 2 == 0 else (2, climb)
        return along(
            held.at[pl.ds(start * height, 2 * height), columns_of(chunk)],
            first_in.at[:, columns_of(chunk)],
            chunk,
            target,
        )

    def second_hop(chunk):
        start, target = (3, climb) if chunk % 2 == 0 else (1, across)
        return along(
            held.at[block(start), columns_of(chunk)],
            second_in.at[:, columns_of(chunk)],
            CHUNKS + chunk,
            target,
        )

    def wide(ref, rows, chunk):
        return ref[rows, columns_of(chunk)].astype(jnp.float32)

    for chunk in range(CHUNKS):

        @pl.loop(0, chunk_width // TILE)
        def _(tile):
            first = pl.multiple_of(chunk * chunk_width + tile * TILE, TILE)
            total = None
            for piece in range(4):
                term = down_product(hidden[piece], downs[piece, pl.ds(first, TILE), :])
                total = term if total is None else total + term
            held[:, pl.ds(first, TILE)] = total.astype(jnp.bfloat16)

        first_hop(chunk).start()
    for chunk in range(CHUNKS):
        first_hop(chunk).wait_recv()
        passing = 3 if chunk % 2 == 0 else 1
        total = wide(held, block(passing), chunk) + wide(first_in, block(1 - chunk % 2), chunk)
        held[block(passing), columns_of(chunk)] = total.astype(jnp.bfloat16)
        second_hop(chunk).start()
    fetch_residual.wait()
    for chunk in range(CHUNKS):
        columns = columns_of(chunk)
        total = (
            residual_ref[:, columns].astype(jnp.float32)
            + wide(held, block(0), chunk)
            + wide(first_in, block(chunk % 2), chunk)
        )
        second_hop(chunk).wait_recv()
        out_ref[:, columns] = (total + second_in[:, columns].astype(jnp.float32)).astype(
            jnp.bfloat16
        )
    for chunk in range(CHUNKS):
        first_hop(chunk).wait_send()
        second_hop(chunk).wait_send()


def mlp(blocks, residual, slices):
    model = blocks.shape[2]
    width = slices.shape[3]
    height = residual.shape[0]
    rows = 4 * height
    vmem = pl.BlockSpec(memory_space=pltpu.VMEM)
    kind = jnp.bfloat16
    return pl.pallas_call(
        mlp_kernel,
        in_specs=[pl.BlockSpec(memory_space=pl.ANY)] * 3,
        out_specs=vmem,
        out_shape=jax.ShapeDtypeStruct((height, model), kind),
        scratch_shapes=[
            pltpu.VMEM((rows, model), kind),
            pltpu.VMEM((height, model), kind),
            pltpu.VMEM((4, model, width), kind),
            pltpu.VMEM((4, model, width), kind),
            pltpu.VMEM((4, model, width), kind),
            pltpu.VMEM((4, rows, width), kind),
            pltpu.VMEM((rows, model), kind),
            pltpu.VMEM((2 * height, model), kind),
            pltpu.VMEM((height, model), kind),
            pltpu.SemaphoreType.DMA((14,)),
            pltpu.SemaphoreType.DMA((2, 2 * CHUNKS)),
        ],
        compiler_params=pltpu.CompilerParams(
            collective_id=2, has_side_effects=True, vmem_limit_bytes=60 * 1024 * 1024
        ),
        cost_estimate=pl.CostEstimate(
            flops=2 * rows * model * width * 12,
            bytes_accessed=12 * model * width * 2 + 2 * rows * model * 2,
            transcendentals=rows * width * 4,
        ),
    )(blocks.reshape(rows, model), residual, slices)


def grouped_layer(
    tokens, rope_pos, inverse, table, local_starts, window, attn_gain, query_key_value_weight,
    out_weight, mlp_gain, gate_up_weight, down_weight, head_index, blocks,
):
    rows_here = tokens.shape[0]
    hidden_here = gate_up_weight.shape[2]
    angles = rope_pos.astype(jnp.float32)[:, None] * inverse[None, :]
    cosine = jnp.cos(angles)
    sine = jnp.sin(angles)

    cosine = jnp.concatenate([cosine, cosine], axis=1).reshape(2, rows_here, HEAD_WIDTH)
    sine = jnp.concatenate([-sine, sine], axis=1).reshape(2, rows_here, HEAD_WIDTH)
    gate_up_rows = gate_up_weight.reshape(gate_up_weight.shape[0], 2 * hidden_here)
    rows, residual, key_cache, value_cache, slices = front(
        tokens, attn_gain[None, :], cosine, sine, table, local_starts, mlp_gain[None, :],
        query_key_value_weight, out_weight, gate_up_rows, down_weight, blocks,
    )
    model = tokens.shape[1]
    output = mlp(rows, residual, slices.reshape(3, 4, model, slices.shape[4]))
    return (output, key_cache, value_cache)


def shards(
    tokens,
    segment_ids,
    lengths,
    deal,
    attn_gain,
    query_key_value_weight,
    out_weight,
    mlp_gain,
    gate_up_weight,
    down_weight,
):
    head_count = lax.axis_size("head")
    head_index = lax.axis_index("head")
    seq_index = lax.axis_index("seq")
    rows_here = tokens.shape[0]
    block_rows = rows_here * head_count
    heads_per_group = QUERY_HEAD_COUNT // KEY_VALUE_HEADS
    groups = query_key_value_weight.shape[1] // ((heads_per_group + 2) * HEAD_WIDTH)
    blocks = deal.shape[0]
    longest = segment_ids.shape[0] // 4
    window = min(blocks, -(-(longest - 1) // block_rows) + 1)
    hidden_here = gate_up_weight.shape[2]
    grouped = head_count == 2 and blocks % GROUP == 0 and hidden_here % (GROUP * 128) == 0
    if not grouped:
        weight_rows = jnp.concatenate(
            [gate_up_weight.reshape(gate_up_weight.shape[0], 2 * hidden_here), down_weight], axis=1
        )
        weights_all = lax.all_gather(weight_rows, "seq", axis=0, tiled=True)
    block_ids = jnp.arange(blocks, dtype=jnp.int32)
    my_block = jnp.sum(jnp.where(block_ids == seq_index, deal, 0))
    stream_pos = my_block * block_rows + jnp.arange(block_rows, dtype=jnp.int32)
    query_segments = lax.dynamic_slice_in_dim(segment_ids, my_block * block_rows, block_rows, 0)
    prompts = jnp.arange(lengths.shape[0], dtype=jnp.int32)
    starts = jnp.sum(jnp.where(prompts[None, :] < prompts[:, None], lengths[None, :], 0), axis=1)
    prompt_hits = query_segments[:, None] == jnp.arange(lengths.shape[0], dtype=jnp.int32)[None, :]
    query_starts = jnp.sum(jnp.where(prompt_hits, starts[None, :], 0), axis=1)
    rope_pos = stream_pos - query_starts
    wanted = jnp.maximum(my_block - (window - 1) + jnp.arange(window, dtype=jnp.int32), 0)
    table = jnp.sum(
        jnp.where(wanted[:, None] == deal[None, :], block_ids[None, :], 0), axis=1
    ).astype(jnp.int32)
    local_starts = (query_starts - (my_block - (window - 1)) * block_rows)[:, None]
    inverse = frequencies(HEAD_WIDTH)
    if grouped:
        return grouped_layer(
            tokens, rope_pos, inverse, table, local_starts, window, attn_gain, query_key_value_weight,
            out_weight, mlp_gain, gate_up_weight, down_weight, head_index, blocks,
        )
    full_rows = jnp.zeros((block_rows, tokens.shape[1]), tokens.dtype)
    full_rows = lax.dynamic_update_slice_in_dim(full_rows, tokens, head_index * rows_here, 0)
    for step in range(1, head_count):
        source = (head_index - step) % head_count
        full_rows = lax.dynamic_update_slice_in_dim(
            full_rows, shift(tokens, step, head_count), source * rows_here, 0
        )
    projected_rows = jnp.dot(
        normalize(full_rows, attn_gain), query_key_value_weight, preferred_element_type=jnp.float32
    )
    projected_rows = projected_rows.reshape(block_rows, groups, heads_per_group + 2, HEAD_WIDTH)
    queries = rotate(projected_rows[:, :, :heads_per_group], rope_pos, inverse).astype(jnp.bfloat16)
    key_matrix = rotate(
        projected_rows[:, :, heads_per_group : heads_per_group + 1], rope_pos, inverse
    )[:, :, 0].astype(jnp.bfloat16)
    value_matrix = projected_rows[:, :, heads_per_group + 1].astype(jnp.bfloat16)
    key_cache = jnp.transpose(key_matrix, (1, 0, 2))
    value_cache = jnp.transpose(value_matrix, (1, 0, 2))
    query_heads = jnp.transpose(queries, (1, 2, 0, 3)).reshape(
        groups, heads_per_group * block_rows, HEAD_WIDTH
    )
    key_value = jnp.stack([key_cache, value_cache])
    pieces = gather_blocks(key_value, blocks)
    attended = attend(query_heads, pieces, table, local_starts, window)
    attended = jnp.transpose(
        attended.reshape(groups, heads_per_group, block_rows, HEAD_WIDTH), (2, 0, 1, 3)
    ).reshape(block_rows, groups * heads_per_group * HEAD_WIDTH)
    part = jnp.dot(attended, out_weight, preferred_element_type=jnp.float32).astype(jnp.bfloat16)
    total_proj = part.astype(jnp.float32)
    for step in range(1, head_count):
        total_proj = total_proj + shift(part, step, head_count).astype(jnp.float32)
    full_residual = (full_rows.astype(jnp.float32) + total_proj).astype(jnp.bfloat16)
    mlp_in = lax.optimization_barrier(normalize(full_residual, mlp_gain))
    residual = lax.dynamic_slice_in_dim(full_residual, head_index * rows_here, rows_here, 0)
    gate = jnp.dot(mlp_in, weights_all[:, :hidden_here], preferred_element_type=jnp.float32)
    up = jnp.dot(
        mlp_in, weights_all[:, hidden_here : 2 * hidden_here], preferred_element_type=jnp.float32
    )
    hidden = (jax.nn.silu(gate) * up).astype(jnp.bfloat16)
    chunks = []
    pieces_down = 3
    width = weights_all.shape[0] // pieces_down
    for number in range(pieces_down):
        columns = slice(number * width, (number + 1) * width)
        terms = down_product(hidden, weights_all[columns, 2 * hidden_here :]).astype(jnp.bfloat16)
        total = residual[:, columns].astype(jnp.float32) + lax.dynamic_slice_in_dim(
            terms, head_index * rows_here, rows_here, 0
        ).astype(jnp.float32)
        for step in range(1, head_count):
            target = (head_index + step) % head_count
            piece = lax.dynamic_slice_in_dim(terms, target * rows_here, rows_here, 0)
            total = total + shift(piece, step, head_count).astype(jnp.float32)
        chunks.append(total.astype(jnp.bfloat16))
    output = jnp.concatenate(chunks, axis=1)
    return (output, key_cache, value_cache)


def solution(mesh):
    placed = (
        P(("seq", "head"), None),
        P(),
        P(),
        P(),
        P(),
        P(None, "head"),
        P("head", None),
        P(),
        P("seq", None, "head"),
        P("seq", "head"),
    )
    return jax.shard_map(
        shards,
        mesh=mesh,
        in_specs=placed,
        out_specs=(P(("seq", "head"), None), P("head", "seq", None), P("head", "seq", None)),
        check_vma=False,
    )
```
